32 devices in a mesh: tm: 4 (over z), rows: 8 (over y, x, core).
Axes of the slice: x: 2, y: 2, z: 4, core: 2. Of those that a mesh axis runs over, the one named last changes fastest.
Arguments:
- frames: bfloat16 [8, 16, 128, 256], P('tm', 'rows'), may hold values from -30 to 30
- frame_counts: int32 [4], replicated, may hold values from 0 to 2, as said below
- norm_gain: float32 [256], replicated, may hold values from 0.5 to 1.5
- norm_bias: float32 [256], replicated, may hold values from -3 to 3
- conv3_weight: bfloat16 [3, 3, 3, 256, 256], replicated, may hold values from -0.078125 to 0.078125
- conv3_bias: float32 [256], replicated, may hold values from -3 to 3
- conv2_weight: bfloat16 [3, 3, 256, 256], replicated, may hold values from -0.125 to 0.125
- conv2_bias: float32 [256], replicated, may hold values from -3 to 3
Outputs:
- decoded: bfloat16 [4, 32, 256, 256], P('tm', 'rows')
The draws below stay inside these ranges and needn't reach their ends.
Inputs may be any that keep to these rules, and one draw needn't show every extreme that they name: `frame_counts`: device d of tm holds the frames starting at the sum of the counts before it, and its first frame index is d or d + 1; the counts sum to 4. Slots at or beyond a device's count hold values that belong to no frame.
All inputs are finite; a program needn't handle non-finite values.
Results may differ from the reference program's by a relative error of at most 0.005.
Values may be sent and summed in bfloat16 or wider, within the bound.
A program may use at most 64 MiB of HBM per device.

```python
import math
import jax
import jax.numpy as jnp
from jax import lax

C = 256
GROUPS = 32
W = 128
FCAP = 2
FRAMES = 4
H = 16
N_TM = 4


def draw_frames(key, part):
    base = jax.random.fold_in(key, 3)
    noise_key, offset_key, channel_key, factor_key, shift_key = jax.random.split(base, 5)
    slot_total = N_TM * FCAP
    full_shape = (slot_total, H, W, C)
    slot_ramp = jnp.arange(slot_total, dtype=jnp.float32) / (slot_total - 1)
    row_ramp = jnp.arange(H, dtype=jnp.float32) / max(H - 1, 1)
    random_level = jax.random.uniform(factor_key, (slot_total, H), jnp.float32, 0.0, 1.0)
    position_scale = jnp.exp(math.log(3.0) * (0.5 * (slot_ramp[:, None] + row_ramp[None, :]) + random_level - 1.0))
    place_offset = jax.random.uniform(shift_key, (slot_total, H), jnp.float32, -1.0, 1.0)
    channel_scale = jnp.exp(jax.random.uniform(channel_key, (C,), jnp.float32, math.log(0.5), math.log(2.0)))
    offsets = jnp.clip(0.5 * jax.random.normal(offset_key, (C,), jnp.float32), -1.5, 1.5)
    noise_field = jnp.clip(jax.random.normal(noise_key, full_shape, jnp.float32), -3.5, 3.5)
    shaped = noise_field * channel_scale + offsets + place_offset[:, :, None, None]
    return (shaped * position_scale[:, :, None, None]).astype(jnp.bfloat16)


def draw_frame_counts(key, part):
    base = jax.random.fold_in(key, 7)
    coin_flips = jax.random.randint(base, (N_TM + 1,), 0, 2)
    boundary = jnp.arange(N_TM + 1)
    lifted = jnp.where((boundary == N_TM - 1) | (boundary == N_TM // 2), 1, coin_flips)
    lifted = jnp.where((boundary == 0) | (boundary == N_TM), 0, lifted)
    return (1 + lifted[1:] - lifted[:-1]).astype(jnp.int32)


def bell_draw(own_key, shape, deviation, limit, kind=jnp.bfloat16):
    values = jax.random.normal(own_key, shape, jnp.float32) * deviation
    return jnp.minimum(jnp.maximum(values, -limit), limit).astype(kind)


def setup_inputs(seed: int = 0) -> dict:
    seeds = jax.random.split(jax.random.key(seed), 9)
    frames = draw_frames(jax.random.fold_in(seeds[8], 71), 0)
    frame_counts = draw_frame_counts(jax.random.fold_in(seeds[8], 71), 0)
    norm_gain = jnp.clip(jax.random.uniform(seeds[2], (C,), jnp.float32, 0.5, 1.5), 0.5, 1.5)
    norm_bias = bell_draw(seeds[3], (C,), 0.5, 3.0, jnp.float32)
    conv3_weight = bell_draw(seeds[4], (3, 3, 3, C, C), (27 * C) ** -0.5, 0.078125)
    conv3_bias = bell_draw(seeds[5], (C,), 0.5, 3.0, jnp.float32)
    conv2_weight = bell_draw(seeds[6], (3, 3, C, C), (9 * C) ** -0.5, 0.125)
    conv2_bias = bell_draw(seeds[7], (C,), 0.5, 3.0, jnp.float32)
    return dict(frames=frames, frame_counts=frame_counts, norm_gain=norm_gain, norm_bias=norm_bias, conv3_weight=conv3_weight, conv3_bias=conv3_bias, conv2_weight=conv2_weight, conv2_bias=conv2_bias)


norm_eps = 1e-06

def reference(frames, frame_counts, norm_gain, norm_bias, conv3_weight, conv3_bias, conv2_weight, conv2_bias):
    starts = (jnp.cumsum(frame_counts) - frame_counts).astype(jnp.int32)
    moments = jnp.arange(FRAMES, dtype=jnp.int32)
    owner_dev = (lax.optimization_barrier(jnp.sum((starts[None, :] <= moments[:, None]).astype(jnp.int32), axis=1)) - 1).astype(jnp.int32)
    position = (owner_dev * FCAP + moments - starts[owner_dev]).astype(jnp.int32)
    clip_frames = frames[position]
    values = clip_frames.astype(jnp.float32)
    grouped = values.reshape(FRAMES, H, W, GROUPS, C // GROUPS)
    group_mean = lax.optimization_barrier(jnp.mean(grouped, axis=(0, 1, 2, 4)))
    group_square = lax.optimization_barrier(jnp.mean(grouped * grouped, axis=(0, 1, 2, 4)))
    inverse = lax.rsqrt(group_square - group_mean * group_mean + norm_eps)
    chan_scale = jnp.repeat(inverse, C // GROUPS) * norm_gain
    chan_shift = norm_bias - jnp.repeat(group_mean * inverse, C // GROUPS) * norm_gain
    hidden = jax.nn.silu(values * chan_scale + chan_shift).astype(jnp.bfloat16)
    padded = jnp.concatenate([hidden[:1], hidden[:1], hidden], axis=0).astype(jnp.float32)
    conv_out = lax.conv_general_dilated(padded[None], conv3_weight.astype(jnp.float32), (1, 1, 1), [(0, 0), (1, 1), (1, 1)], dimension_numbers=('NDHWC', 'DHWIO', 'NDHWC'), precision=lax.Precision.HIGHEST)[0]
    merged = (values + conv_out + conv3_bias).astype(jnp.bfloat16)
    doubled = jnp.repeat(jnp.repeat(merged, 2, axis=1), 2, axis=2).astype(jnp.float32)
    result = lax.conv_general_dilated(doubled, conv2_weight.astype(jnp.float32), (1, 1), [(1, 1), (1, 1)], dimension_numbers=('NHWC', 'HWIO', 'NHWC'), precision=lax.Precision.HIGHEST)
    return (result + conv2_bias).astype(jnp.bfloat16)
```

```python
import functools

import jax
import jax.numpy as jnp
from jax import lax
from jax.experimental import pallas as pl
from jax.experimental.pallas import tpu as pltpu
from jax.sharding import PartitionSpec as P

GROUPS = 32
norm_eps = 1e-06
EDGE = 16
PAD = 8
MESH = pl.DeviceIdType.MESH
f32 = jnp.float32
bf16 = jnp.bfloat16


def group_total(value, width):
    channels = value.shape[1]
    lane = lax.broadcasted_iota(jnp.int32, value.shape, 1)
    step = 1
    while step < width:
        up = pltpu.roll(value, step, 1)
        down = pltpu.roll(value, channels - step, 1)
        value = value + jnp.where((lane // step) % 2 == 1, up, down)
        step *= 2
    return value


def cut(columns, parts):
    while parts > 1 and columns % (EDGE * parts) != 0:
        parts -= 1
    step = columns // parts
    return [(i * step, (i + 1) * step) for i in range(parts)]


def pushed(spans, columns):
    ends = [min(b + EDGE, columns) for _, b in spans]
    ends[-1] = columns
    starts = [0] + ends[:-1]
    return list(zip(starts, ends))


def kernel(
    n_tm, n_rows,
    counts_hbm, frames_hbm, gain_hbm, bias_hbm, w3_hbm, b3_hbm, w2_hbm, b2_hbm,
    out,
    counts, frames, gain, bias, b3, b2,
    w3, w2, cw, xsel, xgot, ext, hid, joined, acc, stage, got, mpad, mjoined, spread,
    stats,
    w_sem, sx, rx, sg, rg, sr, rr, stat_send, stat_recv, ready,
):
    slots, band, columns, channels = frames_hbm.shape
    n_all = n_tm * n_rows
    d = lax.axis_index("tm")
    r = lax.axis_index("rows")
    me = d * n_rows + r
    spans = cut(columns, 4)
    arrivals = pushed(spans, columns)
    parts = len(spans)

    load_counts = pltpu.make_async_copy(counts_hbm, counts, w_sem.at[2])
    load_frames = pltpu.make_async_copy(frames_hbm, frames, w_sem.at[3])
    load3 = pltpu.make_async_copy(w3_hbm, w3, w_sem.at[0])
    load2 = pltpu.make_async_copy(w2_hbm, w2, w_sem.at[1])
    small = [
        pltpu.make_async_copy(source, target, w_sem.at[4 + i])
        for i, (source, target) in enumerate(
            ((gain_hbm, gain), (bias_hbm, bias), (b3_hbm, b3), (b2_hbm, b2))
        )
    ]
    load_counts.start()
    load_frames.start()
    load2.start()
    load3.start()
    for load in small:
        load.start()

    has_next, has_last = d < n_tm - 1, d > 0
    has_above, has_below = r > 0, r < n_rows - 1

    def rank(dd, rr):
        away = dd
        step = 2
        while step < n_rows:
            away = away + (rr // step) % 2
            step *= 2
        return away * n_all + dd * n_rows + rr

    my_rank = rank(d, r)
    barrier = pltpu.get_barrier_semaphore()

    @pl.when(has_last)
    def _():
        pl.semaphore_signal(barrier, inc=1, device_id=(d - 1, r), device_id_type=MESH)

    def other(k):
        at = (me + k) % n_all
        return at // n_rows, at % n_rows

    def greet(k, later):
        dd, rr = other(k)
        after = rank(dd, rr) > my_rank

        @pl.when(after)
        def _():
            pl.semaphore_signal(barrier, inc=1, device_id=(dd, rr), device_id_type=MESH)

        return later + after.astype(jnp.int32)

    n_later = lax.fori_loop(1, n_all, greet, jnp.int32(0))

    load_counts.wait()
    load_frames.wait()
    start = jnp.int32(0)
    for i in range(n_tm):
        start = start + jnp.where(i < d, counts[i], 0)
    live = counts[d]
    own_first = start == d

    for row in range(band):
        xsel[row] = jnp.where(own_first, frames[1, row], frames[0, row])

    sums = jnp.zeros((2, channels), f32)
    for slot in range(slots):
        value = frames[slot].astype(f32).reshape(band * columns // 8, 8, channels)
        total = jnp.sum(jnp.sum(value, axis=0), axis=0, keepdims=True)
        square = jnp.sum(jnp.sum(value * value, axis=0), axis=0, keepdims=True)
        sums = sums + jnp.where(slot < live, jnp.concatenate([total, square], axis=0), 0.0)
    stats[me] = sums

    pl.semaphore_wait(barrier, n_all - 1 - n_later + has_next.astype(jnp.int32))

    def cells(span):
        return pl.ds(span[0], span[1] - span[0])

    def x_copy(c):
        return pltpu.make_async_remote_copy(
            src_ref=xsel.at[:, cells(arrivals[c])], dst_ref=xgot.at[:, cells(arrivals[c])],
            send_sem=sx.at[c], recv_sem=rx.at[c],
            device_id={"tm": (d + 1) % n_tm}, device_id_type=MESH,
        )

    def g_copy(frame, c):
        return pltpu.make_async_remote_copy(
            src_ref=ext.at[frame, :, cells(arrivals[c])],
            dst_ref=ext.at[frame - 1, :, cells(arrivals[c])],
            send_sem=sg.at[frame - 1, c], recv_sem=rg.at[frame - 1, c],
            device_id={"tm": (d + 1) % n_tm}, device_id_type=MESH,
        )

    def r_copy(c, down):
        return pltpu.make_async_remote_copy(
            src_ref=stage.at[down, :, cells(spans[c])], dst_ref=got.at[down, :, cells(spans[c])],
            send_sem=sr.at[c, down], recv_sem=rr.at[c, down],
            device_id={"rows": (r + (1 if down else n_rows - 1)) % n_rows}, device_id_type=MESH,
        )

    def send_stats(k):
        dd, rr = other(k)
        pltpu.make_async_remote_copy(
            src_ref=stats.at[me], dst_ref=stats.at[me], send_sem=stat_send, recv_sem=stat_recv,
            device_id=(dd, rr), device_id_type=MESH,
        ).start()

    @pl.when(has_next)
    def _():
        for c in range(parts):
            x_copy(c).start()

    def announce(k, carry):
        dd, rr = other(k)

        @pl.when(rank(dd, rr) < my_rank)
        def _():
            pl.semaphore_signal(ready, inc=1, device_id=(dd, rr), device_id_type=MESH)

        return carry

    def stats_down(k, carry):
        @pl.when(rank(*other(k)) < my_rank)
        def _():
            send_stats(k)

        return carry

    def stats_up(k, carry):
        @pl.when(rank(*other(k)) > my_rank)
        def _():
            send_stats(k)

        return carry

    lax.fori_loop(1, n_all, announce, 0)
    lax.fori_loop(1, n_all, stats_down, 0)

    load2.wait()
    for phase_row in range(2):
        for tap_row in range(2):
            for phase_col in range(2):
                for tap_col in range(2):
                    rows_of = ((0,), (1, 2)) if phase_row == 0 else ((0, 1), (2,))
                    cols_of = ((0,), (1, 2)) if phase_col == 0 else ((0, 1), (2,))
                    summed = None
                    for a in rows_of[tap_row]:
                        for b in cols_of[tap_col]:
                            part = w2[a, b].astype(f32)
                            summed = part if summed is None else summed + part
                    cw[phase_row, tap_row, phase_col, pl.ds(tap_col * channels, channels), :] = (
                        summed.astype(bf16)
                    )
    for ref in (hid, mpad):
        ref[:, pl.ds(0, PAD)] = jnp.zeros((ref.shape[0], PAD, channels), f32)
        ref[:, pl.ds(PAD + columns, PAD)] = jnp.zeros((ref.shape[0], PAD, channels), f32)

    for c in range(parts):
        at = cells(arrivals[c])

        @pl.when(has_last)
        def _():
            x_copy(c).wait_recv()
            ext[2, :, at] = jnp.where(own_first, frames[0, :, at], xgot[:, at])

        @pl.when(d == 0)
        def _():
            ext[2, :, at] = frames[0, :, at]

        @pl.when(has_next)
        def _():
            g_copy(2, c).start()

        if c == parts // 2:
            @pl.when(n_later > 0)
            def _():
                pl.semaphore_wait(ready, n_later)

            lax.fori_loop(1, n_all, stats_up, 0)

    for c in range(parts):
        @pl.when(has_last)
        def _():
            g_copy(2, c).wait_recv()

        @pl.when(has_last & has_next)
        def _():
            g_copy(1, c).start()

    everyone = stats.at[pl.ds(0, n_all - 1)]
    pltpu.make_async_copy(everyone, everyone, stat_recv).wait()
    whole = jnp.sum(stats[...], axis=0)
    width = channels // GROUPS
    whole = group_total(whole, width) / float(n_all * band * columns * width)
    mean, mean_square = whole[0:1], whole[1:2]
    inverse = lax.rsqrt(mean_square - mean * mean + norm_eps)
    for load in small:
        load.wait()
    scale = inverse * gain[...]
    shift = bias[...] - mean * inverse * gain[...]

    def hide(frame, span):
        value = ext[frame, :, cells(span)].astype(f32) * scale + shift
        value = 0.5 * value * (1.0 + jnp.tanh(0.5 * value))
        hid[:, pl.ds(PAD + span[0], span[1] - span[0])] = value

    def join(source, target, span):
        for i in range(3):
            target[:, cells(span), pl.ds(i * channels, channels)] = (
                source[:, pl.ds(PAD + span[0] + i - 1, span[1] - span[0])].astype(bf16)
            )

    def taps(frame, span):
        held = jnp.maximum(frame, 2 - d)
        size = span[1] - span[0]
        value = joined[held, :, cells(span), :].reshape(band * size, 3 * channels)
        for k in range(3):
            acc[pl.ds(2 - k, band), cells(span)] += jnp.dot(
                value, w3[frame, k], preferred_element_type=f32
            ).reshape(band, size, channels)

    every = (0, columns)
    acc[0] = jnp.zeros((columns, channels), f32)
    acc[band + 1] = jnp.zeros((columns, channels), f32)
    acc[pl.ds(1, band)] = ext[2].astype(f32) + b3[...]
    hide(2, every)
    join(hid, joined.at[2], every)
    load3.wait()
    taps(2, every)

    @pl.when(d >= 1)
    def _():
        hide(1, every)
        join(hid, joined.at[1], every)

    taps(1, every)
    for c in range(parts):
        @pl.when(d >= 2)
        def _():
            g_copy(1, c).wait_recv()
            hide(0, arrivals[c])
            join(hid, joined.at[0], spans[c])

        taps(0, spans[c])
        at = cells(spans[c])
        stage[0, :, at] = acc[pl.ds(0, 2), at].astype(bf16)
        stage[1, :, at] = acc[pl.ds(band, 2), at].astype(bf16)

        @pl.when(has_above)
        def _():
            r_copy(c, 0).start()

        @pl.when(has_below)
        def _():
            r_copy(c, 1).start()

    def upsample(span):
        size = span[1] - span[0]
        for p in range(2):
            for q in range(2):
                summed = b2[...]
                for t in range(2):
                    value = mjoined[pl.ds(p + t, band), cells(span), pl.ds(q * channels, 2 * channels)]
                    summed = summed + jnp.dot(
                        value.reshape(band * size, 2 * channels), cw[p, t, q],
                        preferred_element_type=f32,
                    )
                for i in range(band):
                    for lane in range(0, channels, 128):
                        spread[2 * i + p, lane // 128, pl.ds(2 * span[0] + q, size, stride=2), :] = (
                            summed[i * size : (i + 1) * size, lane : lane + 128]
                        )
            for i in range(band):
                for lane in range(0, channels, 128):
                    to = pl.ds(2 * span[0], 2 * size)
                    out[0, 2 * i + p, to, pl.ds(lane, 128)] = (
                        spread[2 * i + p, lane // 128, to].astype(bf16)
                    )

    done = 0
    for c in range(parts):
        at = cells(spans[c])

        @pl.when(has_below)
        def _():
            r_copy(c, 0).wait_recv()
            acc[pl.ds(band, 2), at] += got[0, :, at].astype(f32)

        @pl.when(has_above)
        def _():
            r_copy(c, 1).wait_recv()
            acc[pl.ds(0, 2), at] += got[1, :, at].astype(f32)

        for j in range(band + 2):
            place = r * band + j - 1
            mpad[j, pl.ds(PAD + spans[c][0], spans[c][1] - spans[c][0])] = jnp.where(
                (place >= 0) & (place < n_rows * band), acc[j, at], 0.0
            )
        if c == parts - 1 or c == parts // 2:
            end = columns if c == parts - 1 else spans[c][1] - EDGE
            join(mpad, mjoined, (done, end))
            upsample((done, end))
            done = end

    pltpu.make_async_copy(everyone, everyone, stat_send).wait()

    @pl.when(has_next)
    def _():
        for c in range(parts):
            x_copy(c).wait_send()
            g_copy(2, c).wait_send()

    @pl.when(has_last & has_next)
    def _():
        for c in range(parts):
            g_copy(1, c).wait_send()

    @pl.when(has_above)
    def _():
        for c in range(parts):
            r_copy(c, 0).wait_send()

    @pl.when(has_below)
    def _():
        for c in range(parts):
            r_copy(c, 1).wait_send()


def body(
    frames, frame_counts, norm_gain, norm_bias, conv3_weight, conv3_bias, conv2_weight, conv2_bias
):
    n_tm, n_rows = lax.axis_size("tm"), lax.axis_size("rows")
    _, band, columns, channels = frames.shape
    parts = len(cut(columns, 4))
    vmem = pl.BlockSpec(memory_space=pltpu.VMEM)
    hbm = pl.BlockSpec(memory_space=pltpu.HBM)
    dma = pltpu.SemaphoreType.DMA
    return pl.pallas_call(
        functools.partial(kernel, n_tm, n_rows),
        out_shape=pltpu.VMEM((1, 2 * band, 2 * columns, channels), bf16),
        in_specs=[
            hbm
        ] * 8,
        out_specs=vmem,
        scratch_shapes=[
            pltpu.SMEM((n_tm,), jnp.int32),
            pltpu.VMEM(frames.shape, bf16),
            pltpu.VMEM((1, channels), f32),
            pltpu.VMEM((1, channels), f32),
            pltpu.VMEM((1, channels), f32),
            pltpu.VMEM((1, channels), f32),
            pltpu.VMEM((3, 3, 3 * channels, channels), bf16),
            pltpu.VMEM((3, 3, channels, channels), bf16),
            pltpu.VMEM((2, 2, 2, 2 * channels, channels), bf16),
            pltpu.VMEM((band, columns, channels), bf16),
            pltpu.VMEM((band, columns, channels), bf16),
            pltpu.VMEM((3, band, columns, channels), bf16),
            pltpu.VMEM((band, columns + 2 * PAD, channels), f32),
            pltpu.VMEM((3, band, columns, 3 * channels), bf16),
            pltpu.VMEM((band + 2, columns, channels), f32),
            pltpu.VMEM((2, 2, columns, channels), bf16),
            pltpu.VMEM((2, 2, columns, channels), bf16),
            pltpu.VMEM((band + 2, columns + 2 * PAD, channels), f32),
            pltpu.VMEM((band + 2, columns, 3 * channels), bf16),
            pltpu.VMEM((2 * band, channels // 128, 2 * columns, 128), f32),
            pltpu.VMEM((n_tm * n_rows, 2, channels), f32),
            dma((8,)),
            dma((parts,)), dma((parts,)),
            dma((2, parts)), dma((2, parts)),
            dma((parts, 2)), dma((parts, 2)),
            dma, dma,
            pltpu.SemaphoreType.REGULAR,
        ],
        compiler_params=pltpu.CompilerParams(
            collective_id=0, has_side_effects=True, vmem_limit_bytes=60000000
        ),
        name="decoder_section",
    )(
        frame_counts, frames, norm_gain[None], norm_bias[None],
        conv3_weight.reshape(3, 3, 3 * channels, channels), conv3_bias[None],
        conv2_weight, conv2_bias[None],
    )


def solution(mesh):
    placed = (P("tm", "rows", None, None), P(), P(), P(), P(), P(), P(), P())
    return jax.shard_map(
        body, mesh=mesh, in_specs=placed, out_specs=P("tm", "rows", None, None), check_vma=False
    )
```

```python
import functools

import jax
import jax.numpy as jnp
from jax import lax
from jax.experimental import pallas as pl
from jax.experimental.pallas import tpu as pltpu
from jax.sharding import PartitionSpec as P

GROUPS = 32
norm_eps = 1e-06
EDGE = 16
PAD = 8
LANES = 128
MESH = pl.DeviceIdType.MESH
f32 = jnp.float32
bf16 = jnp.bfloat16


def group_total(value, width):
    channels = value.shape[1]
    lane = lax.broadcasted_iota(jnp.int32, value.shape, 1)
    step = 1
    while step < width:
        up = pltpu.roll(value, step, 1)
        down = pltpu.roll(value, channels - step, 1)
        value = value + jnp.where((lane // step) % 2 == 1, up, down)
        step *= 2
    return value


def cut(columns, parts):
    while parts > 1 and columns % (EDGE * parts) != 0:
        parts -= 1
    step = columns // parts
    return [(i * step, (i + 1) * step) for i in range(parts)]


def pushed(spans, columns):
    ends = [min(b + EDGE, columns) for _, b in spans]
    ends[-1] = columns
    starts = [0] + ends[:-1]
    return list(zip(starts, ends))


def kernel(
    n_tm, n_rows,
    counts_hbm, frames_hbm, gain_hbm, bias_hbm, w3_hbm, b3_hbm, w2_hbm, b2_hbm,
    out,
    counts, frames, gain, bias, b3, b2,
    w3, w2, cw, xsel, xgot, ext, hid, joined, acc, stage, got, mpad, mjoined, spread,
    stats,
    w_sem, sx, rx, sg, rg, sr, rr, stat_send, stat_recv, ready,
):
    slots, band, columns, channels = frames_hbm.shape
    n_all = n_tm * n_rows
    d = lax.axis_index("tm")
    r = lax.axis_index("rows")
    me = d * n_rows + r
    spans = cut(columns, 4)
    arrivals = pushed(spans, columns)
    parts = len(spans)

    load_counts = pltpu.make_async_copy(counts_hbm, counts, w_sem.at[2])
    load_frames = pltpu.make_async_copy(frames_hbm, frames, w_sem.at[3])
    load3 = pltpu.make_async_copy(w3_hbm, w3, w_sem.at[0])
    load2 = pltpu.make_async_copy(w2_hbm, w2, w_sem.at[1])
    small = [
        pltpu.make_async_copy(source, target, w_sem.at[4 + i])
        for i, (source, target) in enumerate(
            ((gain_hbm, gain), (bias_hbm, bias), (b3_hbm, b3), (b2_hbm, b2))
        )
    ]
    load_counts.start()
    load_frames.start()
    load2.start()
    load3.start()
    for load in small:
        load.start()

    has_next, has_last = d < n_tm - 1, d > 0
    has_above, has_below = r > 0, r < n_rows - 1

    def away(rr):
        steps, step = 0, 2
        while step < n_rows:
            steps = steps + (rr // step) % 2
            step *= 2
        return steps

    def rank(dd, rr):
        return (dd + away(rr)) * n_all + dd * n_rows + rr

    my_rank = rank(d, r)
    barrier = pltpu.get_barrier_semaphore()

    def each(act):
        def plane(dd, carry):
            for at in range(n_rows):
                act(dd, jnp.int32(at))
            return carry

        lax.fori_loop(0, n_tm, plane, 0)

    def later(dd, rr):
        return rank(dd, rr) > my_rank

    def earlier(dd, rr):
        return rank(dd, rr) < my_rank

    n_later = jnp.int32(0)
    for at_tm in range(n_tm):
        for at_rows in range(n_rows):
            n_later = n_later + later(at_tm, at_rows).astype(jnp.int32)

    def greet(dd, rr):
        @pl.when(later(dd, rr))
        def _():
            pl.semaphore_signal(barrier, inc=1, device_id=(dd, rr), device_id_type=MESH)

    @pl.when(has_last)
    def _():
        pl.semaphore_signal(barrier, inc=1, device_id=(d - 1, r), device_id_type=MESH)

    each(greet)
    load_counts.wait()
    load_frames.wait()
    start = jnp.int32(0)
    for i in range(n_tm):
        start = start + jnp.where(i < d, counts[i], 0)
    live = counts[d]
    own_first = start == d

    for row in range(band):
        xsel[row] = jnp.where(own_first, frames[1, row], frames[0, row])

    folds = channels // LANES
    kinds = 2 * folds
    width = channels // GROUPS
    kind_of = lax.broadcasted_iota(jnp.int32, (kinds, LANES), 1) % kinds
    kind_is = kind_of == lax.broadcasted_iota(jnp.int32, (kinds, LANES), 0)
    sums = jnp.zeros((kinds, LANES), f32)
    for slot in range(slots):
        value = frames[slot].astype(f32).reshape(band * columns // 8, 8, channels)
        total = jnp.sum(jnp.sum(value, axis=0), axis=0, keepdims=True)
        square = jnp.sum(jnp.sum(value * value, axis=0), axis=0, keepdims=True)
        parted = [
            value[:, i * LANES : (i + 1) * LANES] for value in (total, square) for i in range(folds)
        ]
        sums = sums + jnp.where(slot < live, jnp.concatenate(parted, axis=0), 0.0)
    sums = jnp.where(kind_is, group_total(sums, width), 0.0)
    stats[me] = jnp.sum(sums, axis=0, keepdims=True)
    pl.semaphore_wait(barrier, n_all - 1 - n_later + has_next.astype(jnp.int32))

    def cells(span):
        return pl.ds(span[0], span[1] - span[0])

    def x_copy(c):
        return pltpu.make_async_remote_copy(
            src_ref=xsel.at[:, cells(arrivals[c])], dst_ref=xgot.at[:, cells(arrivals[c])],
            send_sem=sx.at[c], recv_sem=rx.at[c],
            device_id={"tm": (d + 1) % n_tm}, device_id_type=MESH,
        )

    def g_copy(frame, c):
        return pltpu.make_async_remote_copy(
            src_ref=ext.at[frame, :, cells(arrivals[c])],
            dst_ref=ext.at[frame - 1, :, cells(arrivals[c])],
            send_sem=sg.at[frame - 1, c], recv_sem=rg.at[frame - 1, c],
            device_id={"tm": (d + 1) % n_tm}, device_id_type=MESH,
        )

    def r_copy(c, down):
        return pltpu.make_async_remote_copy(
            src_ref=stage.at[down, :, cells(spans[c])], dst_ref=got.at[down, :, cells(spans[c])],
            send_sem=sr.at[c, down], recv_sem=rr.at[c, down],
            device_id={"rows": (r + (1 if down else n_rows - 1)) % n_rows}, device_id_type=MESH,
        )

    def send_stats(dd, rr):
        pltpu.make_async_remote_copy(
            src_ref=stats.at[me], dst_ref=stats.at[me], send_sem=stat_send, recv_sem=stat_recv,
            device_id=(dd, rr), device_id_type=MESH,
        ).start()

    @pl.when(has_next)
    def _():
        for c in range(parts):
            x_copy(c).start()

    def announce(dd, rr):
        @pl.when(earlier(dd, rr))
        def _():
            pl.semaphore_signal(ready, inc=1, device_id=(dd, rr), device_id_type=MESH)

    each(announce)

    def stats_down(dd, rr):
        @pl.when(earlier(dd, rr))
        def _():
            send_stats(dd, rr)

    def stats_up(dd, rr):
        @pl.when(later(dd, rr))
        def _():
            send_stats(dd, rr)

    each(stats_down)

    load2.wait()
    for phase_row in range(2):
        for tap_row in range(2):
            for phase_col in range(2):
                for tap_col in range(2):
                    rows_of = ((0,), (1, 2)) if phase_row == 0 else ((0, 1), (2,))
                    cols_of = ((0,), (1, 2)) if phase_col == 0 else ((0, 1), (2,))
                    summed = None
                    for a in rows_of[tap_row]:
                        for b in cols_of[tap_col]:
                            part = w2[a, b].astype(f32)
                            summed = part if summed is None else summed + part
                    cw[phase_row, tap_row, phase_col, pl.ds(tap_col * channels, channels), :] = (
                        summed.astype(bf16)
                    )
    for ref in (hid, mpad):
        ref[:, pl.ds(0, PAD)] = jnp.zeros((ref.shape[0], PAD, channels), f32)
        ref[:, pl.ds(PAD + columns, PAD)] = jnp.zeros((ref.shape[0], PAD, channels), f32)

    for c in range(parts):
        at = cells(arrivals[c])

        @pl.when(has_last)
        def _():
            x_copy(c).wait_recv()
            ext[2, :, at] = jnp.where(own_first, frames[0, :, at], xgot[:, at])

        @pl.when(d == 0)
        def _():
            ext[2, :, at] = frames[0, :, at]

        if c == parts // 2 or c == parts - 1:
            @pl.when((d == 0) == (c == parts - 1))
            def _():
                @pl.when(n_later > 0)
                def _():
                    pl.semaphore_wait(ready, n_later)

                each(stats_up)

        @pl.when(d == 0)
        def _():
            x_copy(c).wait_send()

        @pl.when(has_next)
        def _():
            g_copy(2, c).start()

    for c in range(parts):
        @pl.when(has_last)
        def _():
            g_copy(2, c).wait_recv()

        @pl.when(has_last & has_next)
        def _():
            g_copy(1, c).start()

    everyone = stats.at[pl.ds(0, n_all - 1)]
    pltpu.make_async_copy(everyone, everyone, stat_recv).wait()
    whole = jnp.where(kind_is, jnp.sum(stats[...], axis=0), 0.0)
    whole = group_total(whole, width) / float(n_all * band * columns * width * (width // kinds))
    mean, mean_square = (
        jnp.concatenate([whole[i + k : i + k + 1] for i in range(folds)], axis=1) for k in (0, folds)
    )
    inverse = lax.rsqrt(mean_square - mean * mean + norm_eps)
    for load in small:
        load.wait()
    scale = inverse * gain[...]
    shift = bias[...] - mean * inverse * gain[...]

    def hide(frame, span):
        value = ext[frame, :, cells(span)].astype(f32) * scale + shift
        value = 0.5 * value * (1.0 + jnp.tanh(0.5 * value))
        hid[:, pl.ds(PAD + span[0], span[1] - span[0])] = value

    def join(source, target, span):
        for i in range(3):
            target[:, cells(span), pl.ds(i * channels, channels)] = (
                source[:, pl.ds(PAD + span[0] + i - 1, span[1] - span[0])].astype(bf16)
            )

    def taps(frame, span):
        held = jnp.maximum(frame, 2 - d)
        size = span[1] - span[0]
        value = joined[held, :, cells(span), :].reshape(band * size, 3 * channels)
        for k in range(3):
            acc[pl.ds(2 - k, band), cells(span)] += jnp.dot(
                value, w3[frame, k], preferred_element_type=f32
            ).reshape(band, size, channels)

    every = (0, columns)
    acc[0] = jnp.zeros((columns, channels), f32)
    acc[band + 1] = jnp.zeros((columns, channels), f32)
    acc[pl.ds(1, band)] = ext[2].astype(f32) + b3[...]
    hide(2, every)
    join(hid, joined.at[2], every)
    load3.wait()
    taps(2, every)

    @pl.when(d >= 1)
    def _():
        hide(1, every)
        join(hid, joined.at[1], every)

    taps(1, every)
    for c in range(parts):
        @pl.when(d >= 2)
        def _():
            g_copy(1, c).wait_recv()
            hide(0, arrivals[c])
            join(hid, joined.at[0], spans[c])

        taps(0, spans[c])
        at = cells(spans[c])
        stage[0, :, at] = acc[pl.ds(0, 2), at].astype(bf16)
        stage[1, :, at] = acc[pl.ds(band, 2), at].astype(bf16)

        @pl.when(has_above)
        def _():
            r_copy(c, 0).start()

        @pl.when(has_below)
        def _():
            r_copy(c, 1).start()

    def upsample(span):
        size = span[1] - span[0]
        for p in range(2):
            for q in range(2):
                summed = b2[...]
                for t in range(2):
                    value = mjoined[pl.ds(p + t, band), cells(span), pl.ds(q * channels, 2 * channels)]
                    summed = summed + jnp.dot(
                        value.reshape(band * size, 2 * channels), cw[p, t, q],
                        preferred_element_type=f32,
                    )
                for i in range(band):
                    for lane in range(0, channels, 128):
                        spread[2 * i + p, lane // 128, pl.ds(2 * span[0] + q, size, stride=2), :] = (
                            summed[i * size : (i + 1) * size, lane : lane + 128]
                        )
            for i in range(band):
                for lane in range(0, channels, 128):
                    to = pl.ds(2 * span[0], 2 * size)
                    out[0, 2 * i + p, to, pl.ds(lane, 128)] = (
                        spread[2 * i + p, lane // 128, to].astype(bf16)
                    )

    done = 0
    for c in range(parts):
        at = cells(spans[c])

        @pl.when(has_below)
        def _():
            r_copy(c, 0).wait_recv()
            acc[pl.ds(band, 2), at] += got[0, :, at].astype(f32)

        @pl.when(has_above)
        def _():
            r_copy(c, 1).wait_recv()
            acc[pl.ds(0, 2), at] += got[1, :, at].astype(f32)

        for j in range(band + 2):
            place = r * band + j - 1
            mpad[j, pl.ds(PAD + spans[c][0], spans[c][1] - spans[c][0])] = jnp.where(
                (place >= 0) & (place < n_rows * band), acc[j, at], 0.0
            )
        if c == parts - 1 or c == parts // 2:
            end = columns if c == parts - 1 else spans[c][1] - EDGE
            join(mpad, mjoined, (done, end))
            upsample((done, end))
            done = end

    pltpu.make_async_copy(everyone, everyone, stat_send).wait()

    @pl.when(has_next)
    def _():
        for c in range(parts):
            g_copy(2, c).wait_send()

    @pl.when(has_last & has_next)
    def _():
        for c in range(parts):
            x_copy(c).wait_send()
            g_copy(1, c).wait_send()

    @pl.when(has_above)
    def _():
        for c in range(parts):
            r_copy(c, 0).wait_send()

    @pl.when(has_below)
    def _():
        for c in range(parts):
            r_copy(c, 1).wait_send()


def body(
    frames, frame_counts, norm_gain, norm_bias, conv3_weight, conv3_bias, conv2_weight, conv2_bias
):
    n_tm, n_rows = lax.axis_size("tm"), lax.axis_size("rows")
    _, band, columns, channels = frames.shape
    parts = len(cut(columns, 4))
    vmem = pl.BlockSpec(memory_space=pltpu.VMEM)
    hbm = pl.BlockSpec(memory_space=pltpu.HBM)
    dma = pltpu.SemaphoreType.DMA
    return pl.pallas_call(
        functools.partial(kernel, n_tm, n_rows),
        out_shape=pltpu.VMEM((1, 2 * band, 2 * columns, channels), bf16),
        in_specs=[
            hbm
        ] * 8,
        out_specs=vmem,
        scratch_shapes=[
            pltpu.SMEM((n_tm,), jnp.int32),
            pltpu.VMEM(frames.shape, bf16),
            pltpu.VMEM((1, channels), f32),
            pltpu.VMEM((1, channels), f32),
            pltpu.VMEM((1, channels), f32),
            pltpu.VMEM((1, channels), f32),
            pltpu.VMEM((3, 3, 3 * channels, channels), bf16),
            pltpu.VMEM((3, 3, channels, channels), bf16),
            pltpu.VMEM((2, 2, 2, 2 * channels, channels), bf16),
            pltpu.VMEM((band, columns, channels), bf16),
            pltpu.VMEM((band, columns, channels), bf16),
            pltpu.VMEM((3, band, columns, channels), bf16),
            pltpu.VMEM((band, columns + 2 * PAD, channels), f32),
            pltpu.VMEM((3, band, columns, 3 * channels), bf16),
            pltpu.VMEM((band + 2, columns, channels), f32),
            pltpu.VMEM((2, 2, columns, channels), bf16),
            pltpu.VMEM((2, 2, columns, channels), bf16),
            pltpu.VMEM((band + 2, columns + 2 * PAD, channels), f32),
            pltpu.VMEM((band + 2, columns, 3 * channels), bf16),
            pltpu.VMEM((2 * band, channels // 128, 2 * columns, 128), f32),
            pltpu.VMEM((n_tm * n_rows, 1, LANES), f32),
            dma((8,)),
            dma((parts,)), dma((parts,)),
            dma((2, parts)), dma((2, parts)),
            dma((parts, 2)), dma((parts, 2)),
            dma, dma,
            pltpu.SemaphoreType.REGULAR,
        ],
        compiler_params=pltpu.CompilerParams(
            collective_id=0, has_side_effects=True, vmem_limit_bytes=60000000
        ),
        name="decoder_section",
    )(
        frame_counts, frames, norm_gain[None], norm_bias[None],
        conv3_weight.reshape(3, 3, 3 * channels, channels), conv3_bias[None],
        conv2_weight, conv2_bias[None],
    )


def solution(mesh):
    placed = (P("tm", "rows", None, None), P(), P(), P(), P(), P(), P(), P())
    return jax.shard_map(
        body, mesh=mesh, in_specs=placed, out_specs=P("tm", "rows", None, None), check_vma=False
    )
```

```python
import functools

import jax
import jax.numpy as jnp
from jax import lax
from jax.experimental import pallas as pl
from jax.experimental.pallas import tpu as pltpu
from jax.sharding import PartitionSpec as P

GROUPS = 32
norm_eps = 1e-06
EDGE = 16
PAD = 8
LANES = 128
MESH = pl.DeviceIdType.MESH
f32 = jnp.float32
bf16 = jnp.bfloat16


def group_total(value, width):
    channels = value.shape[1]
    lane = lax.broadcasted_iota(jnp.int32, value.shape, 1)
    step = 1
    while step < width:
        up = pltpu.roll(value, step, 1)
        down = pltpu.roll(value, channels - step, 1)
        value = value + jnp.where((lane // step) % 2 == 1, up, down)
        step *= 2
    return value


def cut(columns, parts):
    while parts > 1 and columns % (EDGE * parts) != 0:
        parts -= 1
    step = columns // parts
    return [(i * step, (i + 1) * step) for i in range(parts)]


def pushed(spans, columns):
    ends = [min(b + EDGE, columns) for _, b in spans]
    ends[-1] = columns
    starts = [0] + ends[:-1]
    return list(zip(starts, ends))


def kernel(
    n_tm, n_rows,
    counts_hbm, frames_hbm, gain_hbm, bias_hbm, w3_hbm, b3_hbm, w2_hbm, b2_hbm,
    out,
    counts, frames, gain, bias, b3, b2,
    w3, w2, cw, xsel, xgot, ext, hid, joined, acc, stage, got, mpad, mjoined, spread,
    stats,
    w_sem, sx, rx, sg, rg, sr, rr, stat_send, stat_recv, ready,
):
    slots, band, columns, channels = frames_hbm.shape
    n_all = n_tm * n_rows
    d = lax.axis_index("tm")
    r = lax.axis_index("rows")
    me = d * n_rows + r
    arrivals = pushed(cut(columns, 4), columns)
    parts = len(arrivals)
    spans = cut(columns, 2)

    load_counts = pltpu.make_async_copy(counts_hbm, counts, w_sem.at[2])
    load_frames = pltpu.make_async_copy(frames_hbm, frames, w_sem.at[3])
    load3 = pltpu.make_async_copy(w3_hbm, w3, w_sem.at[0])
    load2 = pltpu.make_async_copy(w2_hbm, w2, w_sem.at[1])
    small = [
        pltpu.make_async_copy(source, target, w_sem.at[4 + i])
        for i, (source, target) in enumerate(
            ((gain_hbm, gain), (bias_hbm, bias), (b3_hbm, b3), (b2_hbm, b2))
        )
    ]
    load_counts.start()
    load_frames.start()
    load2.start()
    load3.start()
    for load in small:
        load.start()

    has_next, has_last = d < n_tm - 1, d > 0
    has_above, has_below = r > 0, r < n_rows - 1

    def away(rr):
        steps, step = 0, 2
        while step < n_rows:
            steps = steps + (rr // step) % 2
            step *= 2
        return steps

    def rank(dd, rr):
        return (dd + away(rr)) * n_all + dd * n_rows + rr

    my_rank = rank(d, r)
    barrier = pltpu.get_barrier_semaphore()

    def each(act):
        def plane(dd, carry):
            for at in range(n_rows):
                act(dd, jnp.int32(at))
            return carry

        lax.fori_loop(0, n_tm, plane, 0)

    def later(dd, rr):
        return rank(dd, rr) > my_rank

    def earlier(dd, rr):
        return rank(dd, rr) < my_rank

    n_later = jnp.int32(0)
    for at_tm in range(n_tm):
        for at_rows in range(n_rows):
            n_later = n_later + later(at_tm, at_rows).astype(jnp.int32)

    def greet(dd, rr):
        @pl.when(later(dd, rr))
        def _():
            pl.semaphore_signal(barrier, inc=1, device_id=(dd, rr), device_id_type=MESH)

    @pl.when(has_last)
    def _():
        pl.semaphore_signal(barrier, inc=1, device_id=(d - 1, r), device_id_type=MESH)

    each(greet)
    load_counts.wait()
    load_frames.wait()
    start = jnp.int32(0)
    for i in range(n_tm):
        start = start + jnp.where(i < d, counts[i], 0)
    live = counts[d]
    own_first = start == d

    for row in range(band):
        xsel[row] = jnp.where(own_first, frames[1, row], frames[0, row])

    folds = channels // LANES
    kinds = 2 * folds
    width = channels // GROUPS
    kind_of = lax.broadcasted_iota(jnp.int32, (kinds, LANES), 1) % kinds
    kind_is = kind_of == lax.broadcasted_iota(jnp.int32, (kinds, LANES), 0)
    sums = jnp.zeros((kinds, LANES), f32)
    for slot in range(slots):
        value = frames[slot].astype(f32).reshape(band * columns // 8, 8, channels)
        total = jnp.sum(jnp.sum(value, axis=0), axis=0, keepdims=True)
        square = jnp.sum(jnp.sum(value * value, axis=0), axis=0, keepdims=True)
        parted = [
            value[:, i * LANES : (i + 1) * LANES] for value in (total, square) for i in range(folds)
        ]
        sums = sums + jnp.where(slot < live, jnp.concatenate(parted, axis=0), 0.0)
    sums = jnp.where(kind_is, group_total(sums, width), 0.0)
    stats[me] = jnp.sum(sums, axis=0, keepdims=True)
    pl.semaphore_wait(barrier, n_all - 1 - n_later + has_next.astype(jnp.int32))

    def cells(span):
        return pl.ds(span[0], span[1] - span[0])

    def x_copy(c):
        return pltpu.make_async_remote_copy(
            src_ref=xsel.at[:, cells(arrivals[c])], dst_ref=xgot.at[:, cells(arrivals[c])],
            send_sem=sx.at[c], recv_sem=rx.at[c],
            device_id={"tm": (d + 1) % n_tm}, device_id_type=MESH,
        )

    def g_copy(frame, c):
        return pltpu.make_async_remote_copy(
            src_ref=ext.at[frame, :, cells(arrivals[c])],
            dst_ref=ext.at[frame - 1, :, cells(arrivals[c])],
            send_sem=sg.at[frame - 1, c], recv_sem=rg.at[frame - 1, c],
            device_id={"tm": (d + 1) % n_tm}, device_id_type=MESH,
        )

    def r_copy(c, down):
        return pltpu.make_async_remote_copy(
            src_ref=stage.at[down, :, cells(spans[c])], dst_ref=got.at[down, :, cells(spans[c])],
            send_sem=sr.at[c, down], recv_sem=rr.at[c, down],
            device_id={"rows": (r + (1 if down else n_rows - 1)) % n_rows}, device_id_type=MESH,
        )

    def send_stats(dd, rr):
        pltpu.make_async_remote_copy(
            src_ref=stats.at[me], dst_ref=stats.at[me], send_sem=stat_send, recv_sem=stat_recv,
            device_id=(dd, rr), device_id_type=MESH,
        ).start()

    @pl.when(has_next)
    def _():
        for c in range(parts):
            x_copy(c).start()

    def announce(dd, rr):
        @pl.when(earlier(dd, rr))
        def _():
            pl.semaphore_signal(ready, inc=1, device_id=(dd, rr), device_id_type=MESH)

    each(announce)

    def stats_down(dd, rr):
        @pl.when(earlier(dd, rr))
        def _():
            send_stats(dd, rr)

    def stats_up(dd, rr):
        @pl.when(later(dd, rr))
        def _():
            send_stats(dd, rr)

    each(stats_down)

    load2.wait()
    for phase_row in range(2):
        for tap_row in range(2):
            for phase_col in range(2):
                for tap_col in range(2):
                    rows_of = ((0,), (1, 2)) if phase_row == 0 else ((0, 1), (2,))
                    cols_of = ((0,), (1, 2)) if phase_col == 0 else ((0, 1), (2,))
                    summed = None
                    for a in rows_of[tap_row]:
                        for b in cols_of[tap_col]:
                            part = w2[a, b].astype(f32)
                            summed = part if summed is None else summed + part
                    cw[phase_row, tap_row, phase_col, pl.ds(tap_col * channels, channels), :] = (
                        summed.astype(bf16)
                    )
    for ref in (hid.at[0], hid.at[1], hid.at[2], mpad):
        ref[:, pl.ds(0, PAD)] = jnp.zeros((ref.shape[0], PAD, channels), f32)
        ref[:, pl.ds(PAD + columns, PAD)] = jnp.zeros((ref.shape[0], PAD, channels), f32)

    @pl.when(r == n_rows - 1)
    def _():
        got[0] = jnp.zeros(got.shape[1:], bf16)

    @pl.when(r == 0)
    def _():
        got[1] = jnp.zeros(got.shape[1:], bf16)

    for c in range(parts):
        at = cells(arrivals[c])

        @pl.when(has_last)
        def _():
            x_copy(c).wait_recv()
            ext[2, :, at] = jnp.where(own_first, frames[0, :, at], xgot[:, at])

        @pl.when(d == 0)
        def _():
            ext[2, :, at] = frames[0, :, at]

        if c == parts // 2 or c == parts - 1:
            @pl.when((d == 0) == (c == parts - 1))
            def _():
                @pl.when(n_later > 0)
                def _():
                    pl.semaphore_wait(ready, n_later)

                each(stats_up)

        @pl.when(d == 0)
        def _():
            x_copy(c).wait_send()

        @pl.when(has_next)
        def _():
            g_copy(2, c).start()

    for c in range(parts):
        @pl.when(has_last)
        def _():
            g_copy(2, c).wait_recv()

        @pl.when(has_last & has_next)
        def _():
            g_copy(1, c).start()

    for load in small:
        load.wait()
    load3.wait()
    acc[0] = jnp.zeros((columns, channels), f32)
    acc[band + 1] = jnp.zeros((columns, channels), f32)
    acc[pl.ds(1, band)] = ext[2].astype(f32) + b3[...]
    everyone = stats.at[pl.ds(0, n_all - 1)]
    pltpu.make_async_copy(everyone, everyone, stat_recv).wait()
    whole = jnp.where(kind_is, jnp.sum(stats[...], axis=0), 0.0)
    whole = group_total(whole, width) / float(n_all * band * columns * width * (width // kinds))
    mean, mean_square = (
        jnp.concatenate([whole[i + k : i + k + 1] for i in range(folds)], axis=1) for k in (0, folds)
    )
    inverse = lax.rsqrt(mean_square - mean * mean + norm_eps)
    scale = inverse * gain[...]
    shift = bias[...] - mean * inverse * gain[...]

    def hide(frame, span):
        value = ext[jnp.maximum(frame, 2 - d), :, cells(span)].astype(f32) * scale + shift
        value = 0.5 * value * (1.0 + jnp.tanh(0.5 * value))
        hid[frame, :, pl.ds(PAD + span[0], span[1] - span[0])] = value

    def join(source, target, span):
        for i in range(3):
            target[:, cells(span), pl.ds(i * channels, channels)] = (
                source[:, pl.ds(PAD + span[0] + i - 1, span[1] - span[0])].astype(bf16)
            )

    def taps(frame, span):
        size = span[1] - span[0]
        value = joined[frame, :, cells(span), :].reshape(band * size, 3 * channels)
        for k in range(3):
            acc[pl.ds(2 - k, band), cells(span)] += jnp.dot(
                value, w3[frame, k], preferred_element_type=f32
            ).reshape(band, size, channels)

    for frame in (2, 1):
        hide(frame, (0, columns))
        join(hid.at[frame], joined.at[frame], (0, columns))
        taps(frame, (0, columns))

    hidden = 0
    for c, span in enumerate(spans):
        upto = columns
        for part, arrival in enumerate(arrivals):
            if hidden <= arrival[0] and (c == len(spans) - 1 or arrival[0] <= span[1]):
                upto = arrival[1]

                @pl.when(d >= 2)
                def _():
                    g_copy(1, part).wait_recv()

        hide(0, (hidden, upto))
        hidden = upto
        join(hid.at[0], joined.at[0], span)
        taps(0, span)
        at = cells(span)
        stage[0, :, at] = acc[pl.ds(0, 2), at].astype(bf16)
        stage[1, :, at] = acc[pl.ds(band, 2), at].astype(bf16)

        @pl.when(has_above)
        def _():
            r_copy(c, 0).start()

        @pl.when(has_below)
        def _():
            r_copy(c, 1).start()

    def upsample(span):
        size = span[1] - span[0]
        for p in range(2):
            for q in range(2):
                summed = b2[...]
                for t in range(2):
                    value = mjoined[pl.ds(p + t, band), cells(span), pl.ds(q * channels, 2 * channels)]
                    summed = summed + jnp.dot(
                        value.reshape(band * size, 2 * channels), cw[p, t, q],
                        preferred_element_type=f32,
                    )
                for i in range(band):
                    for lane in range(0, channels, 128):
                        spread[2 * i + p, lane // 128, pl.ds(2 * span[0] + q, size, stride=2), :] = (
                            summed[i * size : (i + 1) * size, lane : lane + 128]
                        )
            for i in range(band):
                for lane in range(0, channels, 128):
                    to = pl.ds(2 * span[0], 2 * size)
                    out[0, 2 * i + p, to, pl.ds(lane, 128)] = (
                        spread[2 * i + p, lane // 128, to].astype(bf16)
                    )

    done = 0
    for c, span in enumerate(spans):
        at = cells(span)

        @pl.when(has_below)
        def _():
            r_copy(c, 0).wait_recv()

        @pl.when(has_above)
        def _():
            r_copy(c, 1).wait_recv()

        acc[pl.ds(band, 2), at] += got[0, :, at].astype(f32)
        acc[pl.ds(0, 2), at] += got[1, :, at].astype(f32)
        for j in range(band + 2):
            place = r * band + j - 1
            mpad[j, pl.ds(PAD + span[0], span[1] - span[0])] = jnp.where(
                (place >= 0) & (place < n_rows * band), acc[j, at], 0.0
            )
        end = columns if c == len(spans) - 1 else span[1] - EDGE
        join(mpad, mjoined, (done, end))
        upsample((done, end))
        done = end

    pltpu.make_async_copy(everyone, everyone, stat_send).wait()

    @pl.when(has_next)
    def _():
        for c in range(parts):
            g_copy(2, c).wait_send()

    @pl.when(has_last & has_next)
    def _():
        for c in range(parts):
            x_copy(c).wait_send()
            g_copy(1, c).wait_send()

    @pl.when(has_above)
    def _():
        for c in range(len(spans)):
            r_copy(c, 0).wait_send()

    @pl.when(has_below)
    def _():
        for c in range(len(spans)):
            r_copy(c, 1).wait_send()


def body(
    frames, frame_counts, norm_gain, norm_bias, conv3_weight, conv3_bias, conv2_weight, conv2_bias
):
    n_tm, n_rows = lax.axis_size("tm"), lax.axis_size("rows")
    _, band, columns, channels = frames.shape
    parts, steps = len(cut(columns, 4)), len(cut(columns, 2))
    vmem = pl.BlockSpec(memory_space=pltpu.VMEM)
    hbm = pl.BlockSpec(memory_space=pltpu.HBM)
    dma = pltpu.SemaphoreType.DMA
    return pl.pallas_call(
        functools.partial(kernel, n_tm, n_rows),
        out_shape=pltpu.VMEM((1, 2 * band, 2 * columns, channels), bf16),
        in_specs=[
            hbm
        ] * 8,
        out_specs=vmem,
        scratch_shapes=[
            pltpu.SMEM((n_tm,), jnp.int32),
            pltpu.VMEM(frames.shape, bf16),
            pltpu.VMEM((1, channels), f32),
            pltpu.VMEM((1, channels), f32),
            pltpu.VMEM((1, channels), f32),
            pltpu.VMEM((1, channels), f32),
            pltpu.VMEM((3, 3, 3 * channels, channels), bf16),
            pltpu.VMEM((3, 3, channels, channels), bf16),
            pltpu.VMEM((2, 2, 2, 2 * channels, channels), bf16),
            pltpu.VMEM((band, columns, channels), bf16),
            pltpu.VMEM((band, columns, channels), bf16),
            pltpu.VMEM((3, band, columns, channels), bf16),
            pltpu.VMEM((3, band, columns + 2 * PAD, channels), f32),
            pltpu.VMEM((3, band, columns, 3 * channels), bf16),
            pltpu.VMEM((band + 2, columns, channels), f32),
            pltpu.VMEM((2, 2, columns, channels), bf16),
            pltpu.VMEM((2, 2, columns, channels), bf16),
            pltpu.VMEM((band + 2, columns + 2 * PAD, channels), f32),
            pltpu.VMEM((band + 2, columns, 3 * channels), bf16),
            pltpu.VMEM((2 * band, channels // 128, 2 * columns, 128), f32),
            pltpu.VMEM((n_tm * n_rows, 1, LANES), f32),
            dma((8,)),
            dma((parts,)), dma((parts,)),
            dma((2, parts)), dma((2, parts)),
            dma((steps, 2)), dma((steps, 2)),
            dma, dma,
            pltpu.SemaphoreType.REGULAR,
        ],
        compiler_params=pltpu.CompilerParams(
            collective_id=0, has_side_effects=True, vmem_limit_bytes=60000000
        ),
        name="decoder_section",
    )(
        frame_counts, frames, norm_gain[None], norm_bias[None],
        conv3_weight.reshape(3, 3, 3 * channels, channels), conv3_bias[None],
        conv2_weight, conv2_bias[None],
    )


def solution(mesh):
    placed = (P("tm", "rows", None, None), P(), P(), P(), P(), P(), P(), P())
    return jax.shard_map(
        body, mesh=mesh, in_specs=placed, out_specs=P("tm", "rows", None, None), check_vma=False
    )
```

```python
import functools

import jax
import jax.numpy as jnp
from jax import lax
from jax.experimental import pallas as pl
from jax.experimental.pallas import tpu as pltpu
from jax.sharding import PartitionSpec as P

GROUPS = 32
norm_eps = 1e-06
EDGE = 16
PAD = 8
LANES = 128
MESH = pl.DeviceIdType.MESH
f32 = jnp.float32
bf16 = jnp.bfloat16


def group_total(value, width):
    channels = value.shape[1]
    lane = lax.broadcasted_iota(jnp.int32, value.shape, 1)
    step = 1
    while step < width:
        up = pltpu.roll(value, step, 1)
        down = pltpu.roll(value, channels - step, 1)
        value = value + jnp.where((lane // step) % 2 == 1, up, down)
        step *= 2
    return value


def cut(columns, parts):
    while parts > 1 and columns % (EDGE * parts) != 0:
        parts -= 1
    step = columns // parts
    return [(i * step, (i + 1) * step) for i in range(parts)]


def pushed(spans, columns):
    ends = [min(b + EDGE, columns) for _, b in spans]
    ends[-1] = columns
    starts = [0] + ends[:-1]
    return list(zip(starts, ends))


def kernel(
    n_tm, n_rows,
    counts_hbm, frames_hbm, gain_hbm, bias_hbm, w3_hbm, b3_hbm, w2_hbm, b2_hbm,
    out,
    counts, frames, gain, bias, b3, b2,
    w3, w2, cw, xsel, xgot, ext, hid, joined, acc, stage, got, mpad, mjoined, spread,
    stats,
    w_sem, sx, rx, sg, rg, sr, rr, stat_send, stat_recv, ready,
):
    slots, band, columns, channels = frames_hbm.shape
    n_all = n_tm * n_rows
    d = lax.axis_index("tm")
    r = lax.axis_index("rows")
    me = d * n_rows + r
    spans = cut(columns, 4)
    arrivals = pushed(spans, columns)
    parts = len(spans)
    middle = (parts + 1) // 2
    runs = [run for run in ((0, middle), (middle, parts)) if run[0] < run[1]]

    load_counts = pltpu.make_async_copy(counts_hbm, counts, w_sem.at[2])
    load_frames = pltpu.make_async_copy(frames_hbm, frames, w_sem.at[3])
    load3 = pltpu.make_async_copy(w3_hbm, w3, w_sem.at[0])
    load2 = pltpu.make_async_copy(w2_hbm, w2, w_sem.at[1])
    small = [
        pltpu.make_async_copy(source, target, w_sem.at[4 + i])
        for i, (source, target) in enumerate(
            ((gain_hbm, gain), (bias_hbm, bias), (b3_hbm, b3), (b2_hbm, b2))
        )
    ]
    barrier = pltpu.get_barrier_semaphore()

    @pl.when(d > 0)
    def _():
        pl.semaphore_signal(barrier, inc=1, device_id=(d - 1, r), device_id_type=MESH)

    load_counts.start()
    load_frames.start()
    load2.start()
    load3.start()
    for load in small:
        load.start()

    has_next, has_last = d < n_tm - 1, d > 0
    has_above, has_below = r > 0, r < n_rows - 1

    def away(rr):
        steps, step = 0, 2
        while step < n_rows:
            steps = steps + (rr // step) % 2
            step *= 2
        return steps

    def rank(dd, rr):
        return (dd + away(rr)) * n_all + dd * n_rows + rr

    my_rank = rank(d, r)

    def each(act):
        def plane(dd, carry):
            for at in range(n_rows):
                act(dd, jnp.int32(at))
            return carry

        lax.fori_loop(0, n_tm, plane, 0)

    def later(dd, rr):
        return rank(dd, rr) > my_rank

    def earlier(dd, rr):
        return rank(dd, rr) < my_rank

    n_later = jnp.int32(0)
    for at_tm in range(n_tm):
        for at_rows in range(n_rows):
            n_later = n_later + later(at_tm, at_rows).astype(jnp.int32)

    def greet(dd, rr):
        @pl.when(later(dd, rr))
        def _():
            pl.semaphore_signal(barrier, inc=1, device_id=(dd, rr), device_id_type=MESH)

    each(greet)
    load_counts.wait()
    load_frames.wait()
    start = jnp.int32(0)
    for i in range(n_tm):
        start = start + jnp.where(i < d, counts[i], 0)
    live = counts[d]
    own_first = start == d

    for row in range(band):
        xsel[row] = jnp.where(own_first, frames[1, row], frames[0, row])

    folds = channels // LANES
    kinds = 2 * folds
    width = channels // GROUPS
    kind_of = lax.broadcasted_iota(jnp.int32, (kinds, LANES), 1) % kinds
    kind_is = kind_of == lax.broadcasted_iota(jnp.int32, (kinds, LANES), 0)
    sums = jnp.zeros((kinds, LANES), f32)
    for slot in range(slots):
        value = frames[slot].astype(f32).reshape(band * columns // 8, 8, channels)
        total = jnp.sum(jnp.sum(value, axis=0), axis=0, keepdims=True)
        square = jnp.sum(jnp.sum(value * value, axis=0), axis=0, keepdims=True)
        parted = [
            value[:, i * LANES : (i + 1) * LANES] for value in (total, square) for i in range(folds)
        ]
        sums = sums + jnp.where(slot < live, jnp.concatenate(parted, axis=0), 0.0)
    sums = jnp.where(kind_is, group_total(sums, width), 0.0)
    stats[me] = jnp.sum(sums, axis=0, keepdims=True)
    pl.semaphore_wait(barrier, n_all - 1 - n_later + has_next.astype(jnp.int32))

    def cells(span):
        return pl.ds(span[0], span[1] - span[0])

    def x_copy(c):
        return pltpu.make_async_remote_copy(
            src_ref=xsel.at[:, cells(arrivals[c])], dst_ref=xgot.at[:, cells(arrivals[c])],
            send_sem=sx.at[c], recv_sem=rx.at[c],
            device_id={"tm": (d + 1) % n_tm}, device_id_type=MESH,
        )

    def g_copy(frame, c):
        return pltpu.make_async_remote_copy(
            src_ref=ext.at[frame, :, cells(arrivals[c])],
            dst_ref=ext.at[frame - 1, :, cells(arrivals[c])],
            send_sem=sg.at[frame - 1, c], recv_sem=rg.at[frame - 1, c],
            device_id={"tm": (d + 1) % n_tm}, device_id_type=MESH,
        )

    def r_copy(c, down):
        return pltpu.make_async_remote_copy(
            src_ref=stage.at[down, :, cells(spans[c])], dst_ref=got.at[down, :, cells(spans[c])],
            send_sem=sr.at[c, down], recv_sem=rr.at[c, down],
            device_id={"rows": (r + (1 if down else n_rows - 1)) % n_rows}, device_id_type=MESH,
        )

    def send_stats(dd, rr):
        pltpu.make_async_remote_copy(
            src_ref=stats.at[me], dst_ref=stats.at[me], send_sem=stat_send, recv_sem=stat_recv,
            device_id=(dd, rr), device_id_type=MESH,
        ).start()

    @pl.when(has_next)
    def _():
        for c in range(parts):
            x_copy(c).start()

    def announce(dd, rr):
        @pl.when(earlier(dd, rr))
        def _():
            pl.semaphore_signal(ready.at[d], inc=1, device_id=(dd, rr), device_id_type=MESH)

    each(announce)

    def stats_down(dd, rr):
        @pl.when(earlier(dd, rr))
        def _():
            send_stats(dd, rr)

    def stats_up(dd):
        ahead = jnp.int32(0)
        for at_rows in range(n_rows):
            ahead = ahead + later(dd, at_rows).astype(jnp.int32)

        @pl.when(ahead > 0)
        def _():
            pl.semaphore_wait(ready.at[dd], ahead)
            for at_rows in range(n_rows):
                @pl.when(later(dd, at_rows))
                def _():
                    send_stats(dd, jnp.int32(at_rows))

    def stats_away(dd, carry):
        @pl.when(dd != d)
        def _():
            stats_up(dd)

        return carry

    each(stats_down)

    load2.wait()
    for phase_row in range(2):
        for tap_row in range(2):
            for phase_col in range(2):
                for tap_col in range(2):
                    rows_of = ((0,), (1, 2)) if phase_row == 0 else ((0, 1), (2,))
                    cols_of = ((0,), (1, 2)) if phase_col == 0 else ((0, 1), (2,))
                    summed = None
                    for a in rows_of[tap_row]:
                        for b in cols_of[tap_col]:
                            part = w2[a, b].astype(f32)
                            summed = part if summed is None else summed + part
                    cw[phase_row, tap_row, phase_col, pl.ds(tap_col * channels, channels), :] = (
                        summed.astype(bf16)
                    )
    load3.wait()

    @pl.when(d < 2)
    def _():
        for k in range(3):
            w3[1, k] = (w3[1, k].astype(f32) + w3[0, k].astype(f32)).astype(bf16)

    for ref in (hid.at[0], hid.at[1], hid.at[2], mpad):
        ref[:, pl.ds(0, PAD)] = jnp.zeros((ref.shape[0], PAD, channels), f32)
        ref[:, pl.ds(PAD + columns, PAD)] = jnp.zeros((ref.shape[0], PAD, channels), f32)

    @pl.when(r == n_rows - 1)
    def _():
        got[0] = jnp.zeros(got.shape[1:], bf16)

    @pl.when(r == 0)
    def _():
        got[1] = jnp.zeros(got.shape[1:], bf16)

    for c in range(parts):
        at = cells(arrivals[c])

        @pl.when(has_last)
        def _():
            x_copy(c).wait_recv()
            ext[2, :, at] = jnp.where(own_first, frames[0, :, at], xgot[:, at])

        @pl.when(d == 0)
        def _():
            ext[2, :, at] = frames[0, :, at]

        if c == 0:
            stats_up(d)
        if c == parts // 4 or c == parts // 2:
            @pl.when((d == 0) == (c == parts // 2))
            def _():
                lax.fori_loop(0, n_tm, stats_away, 0)

        @pl.when(d == 0)
        def _():
            x_copy(c).wait_send()

        @pl.when(has_next)
        def _():
            g_copy(2, c).start()

    def pass_on(first, last):
        for c in range(first, last):
            g_copy(2, c).wait_recv()

            @pl.when(has_next)
            def _():
                g_copy(1, c).start()

    @pl.when(has_last)
    def _():
        pass_on(0, parts)

    for load in small:
        load.wait()
    acc[0] = jnp.zeros((columns, channels), f32)
    acc[band + 1] = jnp.zeros((columns, channels), f32)
    acc[pl.ds(1, band)] = ext[2].astype(f32) + b3[...]
    everyone = stats.at[pl.ds(0, n_all - 1)]
    pltpu.make_async_copy(everyone, everyone, stat_recv).wait()
    whole = jnp.where(kind_is, jnp.sum(stats[...], axis=0), 0.0)
    whole = group_total(whole, width) / float(n_all * band * columns * width * (width // kinds))
    mean, mean_square = (
        jnp.concatenate([whole[i + k : i + k + 1] for i in range(folds)], axis=1) for k in (0, folds)
    )
    inverse = lax.rsqrt(mean_square - mean * mean + norm_eps)
    scale = inverse * gain[...]
    shift = bias[...] - mean * inverse * gain[...]

    def hide(frame, span):
        value = ext[jnp.maximum(frame, 2 - d), :, cells(span)].astype(f32) * scale + shift
        value = 0.5 * value * (1.0 + jnp.tanh(0.5 * value))
        hid[frame, :, pl.ds(PAD + span[0], span[1] - span[0])] = value

    def join(source, target, span):
        for i in range(3):
            target[:, cells(span), pl.ds(i * channels, channels)] = (
                source[:, pl.ds(PAD + span[0] + i - 1, span[1] - span[0])].astype(bf16)
            )

    def taps(frame, held, span):
        size = span[1] - span[0]
        value = joined[held, :, cells(span), :].reshape(band * size, 3 * channels)
        for k in range(3):
            acc[pl.ds(2 - k, band), cells(span)] += jnp.dot(
                value, w3[frame, k], preferred_element_type=f32
            ).reshape(band, size, channels)

    def send_edges(first, last):
        at = cells((spans[first][0], spans[last - 1][1]))
        stage[0, :, at] = acc[pl.ds(0, 2), at].astype(bf16)
        stage[1, :, at] = acc[pl.ds(band, 2), at].astype(bf16)

        @pl.when(has_above)
        def _():
            for c in range(first, last):
                r_copy(c, 0).start()

        @pl.when(has_below)
        def _():
            for c in range(first, last):
                r_copy(c, 1).start()

    every = (0, columns)
    hide(2, every)
    join(hid.at[2], joined.at[2], every)
    taps(2, 2, every)

    def covered(spans, run):
        return spans[run[0]][0], spans[run[1] - 1][1]

    @pl.when(d < 2)
    def _():
        for run in runs:
            hide(1, covered(arrivals, run))
            join(hid.at[1], joined.at[1], covered(spans, run))
            taps(1, 1, covered(spans, run))
            send_edges(*run)

    @pl.when(d >= 2)
    def _():
        hide(1, every)
        join(hid.at[1], joined.at[1], every)
        taps(1, 1, every)
        for run in runs:
            for c in range(*run):
                g_copy(1, c).wait_recv()
            hide(0, covered(arrivals, run))
            join(hid.at[0], joined.at[0], covered(spans, run))
            taps(0, 0, covered(spans, run))
            send_edges(*run)

    def upsample(span):
        size = span[1] - span[0]
        for p in range(2):
            for q in range(2):
                summed = b2[...]
                for t in range(2):
                    value = mjoined[pl.ds(p + t, band), cells(span), pl.ds(q * channels, 2 * channels)]
                    summed = summed + jnp.dot(
                        value.reshape(band * size, 2 * channels), cw[p, t, q],
                        preferred_element_type=f32,
                    )
                for i in range(band):
                    for lane in range(0, channels, 128):
                        spread[2 * i + p, lane // 128, pl.ds(2 * span[0] + q, size, stride=2), :] = (
                            summed[i * size : (i + 1) * size, lane : lane + 128]
                        )
            for i in range(band):
                for lane in range(0, channels, 128):
                    to = pl.ds(2 * span[0], 2 * size)
                    out[0, 2 * i + p, to, pl.ds(lane, 128)] = (
                        spread[2 * i + p, lane // 128, to].astype(bf16)
                    )

    done = 0
    for c, span in enumerate(spans):
        at = cells(span)

        @pl.when(has_below)
        def _():
            r_copy(c, 0).wait_recv()

        @pl.when(has_above)
        def _():
            r_copy(c, 1).wait_recv()

        acc[pl.ds(band, 2), at] += got[0, :, at].astype(f32)
        acc[pl.ds(0, 2), at] += got[1, :, at].astype(f32)
        for j in range(band + 2):
            place = r * band + j - 1
            mpad[j, pl.ds(PAD + span[0], span[1] - span[0])] = jnp.where(
                (place >= 0) & (place < n_rows * band), acc[j, at], 0.0
            )
        if c == middle - 1 or c == parts - 1:
            end = columns if c == parts - 1 else span[1] - EDGE
            join(mpad, mjoined, (done, end))
            upsample((done, end))
            done = end

    pltpu.make_async_copy(everyone, everyone, stat_send).wait()

    @pl.when(has_next)
    def _():
        for c in range(parts):
            g_copy(2, c).wait_send()

    @pl.when(has_last & has_next)
    def _():
        for c in range(parts):
            x_copy(c).wait_send()
            g_copy(1, c).wait_send()

    @pl.when(has_above)
    def _():
        for c in range(parts):
            r_copy(c, 0).wait_send()

    @pl.when(has_below)
    def _():
        for c in range(parts):
            r_copy(c, 1).wait_send()


def body(
    frames, frame_counts, norm_gain, norm_bias, conv3_weight, conv3_bias, conv2_weight, conv2_bias
):
    n_tm, n_rows = lax.axis_size("tm"), lax.axis_size("rows")
    _, band, columns, channels = frames.shape
    parts = len(cut(columns, 4))
    vmem = pl.BlockSpec(memory_space=pltpu.VMEM)
    hbm = pl.BlockSpec(memory_space=pltpu.HBM)
    dma = pltpu.SemaphoreType.DMA
    return pl.pallas_call(
        functools.partial(kernel, n_tm, n_rows),
        out_shape=pltpu.VMEM((1, 2 * band, 2 * columns, channels), bf16),
        in_specs=[
            hbm
        ] * 8,
        out_specs=vmem,
        scratch_shapes=[
            pltpu.SMEM((n_tm,), jnp.int32),
            pltpu.VMEM(frames.shape, bf16),
            pltpu.VMEM((1, channels), f32),
            pltpu.VMEM((1, channels), f32),
            pltpu.VMEM((1, channels), f32),
            pltpu.VMEM((1, channels), f32),
            pltpu.VMEM((3, 3, 3 * channels, channels), bf16),
            pltpu.VMEM((3, 3, channels, channels), bf16),
            pltpu.VMEM((2, 2, 2, 2 * channels, channels), bf16),
            pltpu.VMEM((band, columns, channels), bf16),
            pltpu.VMEM((band, columns, channels), bf16),
            pltpu.VMEM((3, band, columns, channels), bf16),
            pltpu.VMEM((3, band, columns + 2 * PAD, channels), f32),
            pltpu.VMEM((3, band, columns, 3 * channels), bf16),
            pltpu.VMEM((band + 2, columns, channels), f32),
            pltpu.VMEM((2, 2, columns, channels), bf16),
            pltpu.VMEM((2, 2, columns, channels), bf16),
            pltpu.VMEM((band + 2, columns + 2 * PAD, channels), f32),
            pltpu.VMEM((band + 2, columns, 3 * channels), bf16),
            pltpu.VMEM((2 * band, channels // 128, 2 * columns, 128), f32),
            pltpu.VMEM((n_tm * n_rows, 1, LANES), f32),
            dma((8,)),
            dma((parts,)), dma((parts,)),
            dma((2, parts)), dma((2, parts)),
            dma((parts, 2)), dma((parts, 2)),
            dma, dma,
            pltpu.SemaphoreType.REGULAR((n_tm,)),
        ],
        compiler_params=pltpu.CompilerParams(
            collective_id=0, has_side_effects=True, vmem_limit_bytes=60000000
        ),
        name="decoder_section",
    )(
        frame_counts, frames, norm_gain[None], norm_bias[None],
        conv3_weight.reshape(3, 3, 3 * channels, channels), conv3_bias[None],
        conv2_weight, conv2_bias[None],
    )


def solution(mesh):
    placed = (P("tm", "rows", None, None), P(), P(), P(), P(), P(), P(), P())
    return jax.shard_map(
        body, mesh=mesh, in_specs=placed, out_specs=P("tm", "rows", None, None), check_vma=False
    )
```

```python
import functools

import jax
import jax.numpy as jnp
from jax import lax
from jax.experimental import pallas as pl
from jax.experimental.pallas import tpu as pltpu
from jax.sharding import PartitionSpec as P

GROUPS = 32
norm_eps = 1e-06
EDGE = 16
PAD = 8
LANES = 128
MESH = pl.DeviceIdType.MESH
f32 = jnp.float32
bf16 = jnp.bfloat16


def group_total(value, width):
    channels = value.shape[1]
    lane = lax.broadcasted_iota(jnp.int32, value.shape, 1)
    step = 1
    while step < width:
        up = pltpu.roll(value, step, 1)
        down = pltpu.roll(value, channels - step, 1)
        value = value + jnp.where((lane // step) % 2 == 1, up, down)
        step *= 2
    return value


def cut(columns, parts):
    while parts > 1 and columns % (EDGE * parts) != 0:
        parts -= 1
    step = columns // parts
    return [(i * step, (i + 1) * step) for i in range(parts)]


def pushed(spans, columns):
    ends = [min(b + EDGE, columns) for _, b in spans]
    ends[-1] = columns
    starts = [0] + ends[:-1]
    return list(zip(starts, ends))


def kernel(
    n_tm, n_rows,
    counts_hbm, frames_hbm, gain_hbm, bias_hbm, w3_hbm, b3_hbm, w2_hbm, b2_hbm,
    out,
    counts, frames, gain, bias, b3, b2,
    w3, w2, cw, xsel, xgot, ext, hid, joined, acc, stage, got, mpad, mjoined, spread,
    stats,
    w_sem, sx, rx, sg, rg, sr, rr, stat_send, stat_recv, ready,
):
    slots, band, columns, channels = frames_hbm.shape
    n_all = n_tm * n_rows
    d = lax.axis_index("tm")
    r = lax.axis_index("rows")
    me = d * n_rows + r
    spans = cut(columns, 4)
    arrivals = pushed(spans, columns)
    parts = len(spans)
    middle = (parts + 1) // 2
    runs = [run for run in ((0, middle), (middle, parts)) if run[0] < run[1]]

    load_counts = pltpu.make_async_copy(counts_hbm, counts, w_sem.at[2])
    load_frames = pltpu.make_async_copy(frames_hbm, frames, w_sem.at[3])
    load3 = pltpu.make_async_copy(w3_hbm, w3, w_sem.at[0])
    load2 = pltpu.make_async_copy(w2_hbm, w2, w_sem.at[1])
    small = [
        pltpu.make_async_copy(source, target, w_sem.at[4 + i])
        for i, (source, target) in enumerate(
            ((gain_hbm, gain), (bias_hbm, bias), (b3_hbm, b3), (b2_hbm, b2))
        )
    ]
    barrier = pltpu.get_barrier_semaphore()

    @pl.when(d > 0)
    def _():
        pl.semaphore_signal(barrier, inc=1, device_id=(d - 1, r), device_id_type=MESH)

    load_counts.start()
    load_frames.start()
    load2.start()
    load3.start()
    for load in small:
        load.start()

    has_next, has_last = d < n_tm - 1, d > 0
    has_above, has_below = r > 0, r < n_rows - 1

    def away(rr):
        steps, step = 0, 2
        while step < n_rows:
            steps = steps + (rr // step) % 2
            step *= 2
        return steps

    def rank(dd, rr):
        return (dd + away(rr)) * n_all + dd * n_rows + rr

    my_rank = rank(d, r)

    def each(act):
        def plane(dd, carry):
            for at in range(n_rows):
                act(dd, jnp.int32(at))
            return carry

        lax.fori_loop(0, n_tm, plane, 0)

    def later(dd, rr):
        return rank(dd, rr) > my_rank

    def earlier(dd, rr):
        return rank(dd, rr) < my_rank

    n_later = jnp.int32(0)
    for at_tm in range(n_tm):
        for at_rows in range(n_rows):
            n_later = n_later + later(at_tm, at_rows).astype(jnp.int32)

    def greet(dd, rr):
        @pl.when(later(dd, rr))
        def _():
            pl.semaphore_signal(barrier, inc=1, device_id=(dd, rr), device_id_type=MESH)

    each(greet)
    load_counts.wait()
    load_frames.wait()
    start = jnp.int32(0)
    for i in range(n_tm):
        start = start + jnp.where(i < d, counts[i], 0)
    live = counts[d]
    own_first = start == d

    for row in range(band):
        xsel[row] = jnp.where(own_first, frames[1, row], frames[0, row])

    folds = channels // LANES
    kinds = 2 * folds
    width = channels // GROUPS
    kind_of = lax.broadcasted_iota(jnp.int32, (kinds, LANES), 1) % kinds
    kind_is = kind_of == lax.broadcasted_iota(jnp.int32, (kinds, LANES), 0)
    sums = jnp.zeros((kinds, LANES), f32)
    for slot in range(slots):
        value = frames[slot].astype(f32).reshape(band * columns // 8, 8, channels)
        total = jnp.sum(jnp.sum(value, axis=0), axis=0, keepdims=True)
        square = jnp.sum(jnp.sum(value * value, axis=0), axis=0, keepdims=True)
        parted = [
            value[:, i * LANES : (i + 1) * LANES] for value in (total, square) for i in range(folds)
        ]
        sums = sums + jnp.where(slot < live, jnp.concatenate(parted, axis=0), 0.0)
    sums = jnp.where(kind_is, group_total(sums, width), 0.0)
    stats[me] = jnp.sum(sums, axis=0, keepdims=True)
    pl.semaphore_wait(barrier, n_all - 1 - n_later + has_next.astype(jnp.int32))

    def cells(span):
        return pl.ds(span[0], span[1] - span[0])

    def x_copy(c):
        return pltpu.make_async_remote_copy(
            src_ref=xsel.at[:, cells(arrivals[c])], dst_ref=xgot.at[:, cells(arrivals[c])],
            send_sem=sx.at[c], recv_sem=rx.at[c],
            device_id={"tm": (d + 1) % n_tm}, device_id_type=MESH,
        )

    def g_copy(frame, c):
        return pltpu.make_async_remote_copy(
            src_ref=ext.at[frame, :, cells(arrivals[c])],
            dst_ref=ext.at[frame - 1, :, cells(arrivals[c])],
            send_sem=sg.at[frame - 1, c], recv_sem=rg.at[frame - 1, c],
            device_id={"tm": (d + 1) % n_tm}, device_id_type=MESH,
        )

    def r_copy(c, down):
        return pltpu.make_async_remote_copy(
            src_ref=stage.at[down, :, cells(spans[c])], dst_ref=got.at[down, :, cells(spans[c])],
            send_sem=sr.at[c, down], recv_sem=rr.at[c, down],
            device_id={"rows": (r + (1 if down else n_rows - 1)) % n_rows}, device_id_type=MESH,
        )

    def send_stats(dd, rr):
        pltpu.make_async_remote_copy(
            src_ref=stats.at[me], dst_ref=stats.at[me], send_sem=stat_send, recv_sem=stat_recv,
            device_id=(dd, rr), device_id_type=MESH,
        ).start()

    @pl.when(has_next)
    def _():
        for c in range(parts):
            x_copy(c).start()

    def announce(dd, rr):
        @pl.when(earlier(dd, rr))
        def _():
            pl.semaphore_signal(ready.at[d], inc=1, device_id=(dd, rr), device_id_type=MESH)

    each(announce)

    def stats_down(dd, rr):
        @pl.when(earlier(dd, rr))
        def _():
            send_stats(dd, rr)

    def stats_up(dd):
        ahead = jnp.int32(0)
        for at_rows in range(n_rows):
            ahead = ahead + later(dd, at_rows).astype(jnp.int32)

        @pl.when(ahead > 0)
        def _():
            pl.semaphore_wait(ready.at[dd], ahead)
            for at_rows in range(n_rows):
                @pl.when(later(dd, at_rows))
                def _():
                    send_stats(dd, jnp.int32(at_rows))

    def stats_away(dd, carry):
        @pl.when(dd != d)
        def _():
            stats_up(dd)

        return carry

    each(stats_down)

    load2.wait()
    for phase_row in range(2):
        for tap_row in range(2):
            for phase_col in range(2):
                for tap_col in range(2):
                    rows_of = ((0,), (1, 2)) if phase_row == 0 else ((0, 1), (2,))
                    cols_of = ((0,), (1, 2)) if phase_col == 0 else ((0, 1), (2,))
                    summed = None
                    for a in rows_of[tap_row]:
                        for b in cols_of[tap_col]:
                            part = w2[a, b].astype(f32)
                            summed = part if summed is None else summed + part
                    cw[phase_row, tap_row, phase_col, pl.ds(tap_col * channels, channels), :] = (
                        summed.astype(bf16)
                    )
    load3.wait()

    @pl.when(d < 2)
    def _():
        for k in range(3):
            w3[1, k] = (w3[1, k].astype(f32) + w3[0, k].astype(f32)).astype(bf16)

    for ref in (hid.at[0], hid.at[1], hid.at[2], mpad):
        ref[:, pl.ds(0, PAD)] = jnp.zeros((ref.shape[0], PAD, channels), f32)
        ref[:, pl.ds(PAD + columns, PAD)] = jnp.zeros((ref.shape[0], PAD, channels), f32)

    @pl.when(r == n_rows - 1)
    def _():
        got[0] = jnp.zeros(got.shape[1:], bf16)

    @pl.when(r == 0)
    def _():
        got[1] = jnp.zeros(got.shape[1:], bf16)

    for c in range(parts):
        at = cells(arrivals[c])

        @pl.when(has_last)
        def _():
            x_copy(c).wait_recv()
            ext[2, :, at] = jnp.where(own_first, frames[0, :, at], xgot[:, at])

        @pl.when(d == 0)
        def _():
            ext[2, :, at] = frames[0, :, at]

        if c == 0:
            stats_up(d)
        if c == parts // 4 or c == parts // 2:
            @pl.when((d == 0) == (c == parts // 2))
            def _():
                lax.fori_loop(0, n_tm, stats_away, 0)

        @pl.when(d == 0)
        def _():
            x_copy(c).wait_send()

        @pl.when(has_next)
        def _():
            g_copy(2, c).start()

    def pass_on(first, last):
        for c in range(first, last):
            g_copy(2, c).wait_recv()

            @pl.when(has_next)
            def _():
                g_copy(1, c).start()

    @pl.when(has_last)
    def _():
        pass_on(0, parts)

    for load in small:
        load.wait()
    acc[0] = jnp.zeros((columns, channels), f32)
    acc[band + 1] = jnp.zeros((columns, channels), f32)
    acc[pl.ds(1, band)] = ext[2].astype(f32) + b3[...]
    everyone = stats.at[pl.ds(0, n_all - 1)]
    pltpu.make_async_copy(everyone, everyone, stat_recv).wait()
    whole = jnp.where(kind_is, jnp.sum(stats[...], axis=0), 0.0)
    whole = group_total(whole, width) / float(n_all * band * columns * width * (width // kinds))
    mean, mean_square = (
        jnp.concatenate([whole[i + k : i + k + 1] for i in range(folds)], axis=1) for k in (0, folds)
    )
    inverse = lax.rsqrt(mean_square - mean * mean + norm_eps)
    scale = inverse * gain[...]
    shift = bias[...] - mean * inverse * gain[...]

    def hide(frame, span):
        value = ext[jnp.maximum(frame, 2 - d), :, cells(span)].astype(f32) * scale + shift
        value = 0.5 * value * (1.0 + jnp.tanh(0.5 * value))
        hid[frame, :, pl.ds(PAD + span[0], span[1] - span[0])] = value

    def join(source, target, span):
        for i in range(3):
            target[:, cells(span), pl.ds(i * channels, channels)] = (
                source[:, pl.ds(PAD + span[0] + i - 1, span[1] - span[0])].astype(bf16)
            )

    def taps(frame, held, span, rows=(0, 1, 2)):
        size = span[1] - span[0]
        value = joined[held, :, cells(span), :].reshape(band * size, 3 * channels)
        for k in rows:
            acc[pl.ds(2 - k, band), cells(span)] += jnp.dot(
                value, w3[frame, k], preferred_element_type=f32
            ).reshape(band, size, channels)

    def send_edge(first, last, down):
        at = cells((spans[first][0], spans[last - 1][1]))
        stage[down, :, at] = acc[pl.ds(band if down else 0, 2), at].astype(bf16)

        @pl.when(has_below if down else has_above)
        def _():
            for c in range(first, last):
                r_copy(c, down).start()

    def last_taps(frame, held, span, run):
        @pl.when(r % 2 == 0)
        def _():
            taps(frame, held, span, (2, 1))
            send_edge(*run, 0)
            taps(frame, held, span, (0,))
            send_edge(*run, 1)

        @pl.when(r % 2 == 1)
        def _():
            taps(frame, held, span, (0, 1))
            send_edge(*run, 1)
            taps(frame, held, span, (2,))
            send_edge(*run, 0)

    every = (0, columns)
    hide(2, every)
    join(hid.at[2], joined.at[2], every)
    taps(2, 2, every)

    def covered(spans, run):
        return spans[run[0]][0], spans[run[1] - 1][1]

    @pl.when(d < 2)
    def _():
        for run in runs:
            hide(1, covered(arrivals, run))
            join(hid.at[1], joined.at[1], covered(spans, run))
            last_taps(1, 1, covered(spans, run), run)

    @pl.when(d >= 2)
    def _():
        hide(1, every)
        join(hid.at[1], joined.at[1], every)
        taps(1, 1, every)
        for run in runs:
            for c in range(*run):
                g_copy(1, c).wait_recv()
            hide(0, covered(arrivals, run))
            join(hid.at[0], joined.at[0], covered(spans, run))
            last_taps(0, 0, covered(spans, run), run)

    def upsample(span):
        size = span[1] - span[0]
        for p in range(2):
            for q in range(2):
                summed = b2[...]
                for t in range(2):
                    value = mjoined[pl.ds(p + t, band), cells(span), pl.ds(q * channels, 2 * channels)]
                    summed = summed + jnp.dot(
                        value.reshape(band * size, 2 * channels), cw[p, t, q],
                        preferred_element_type=f32,
                    )
                for i in range(band):
                    for lane in range(0, channels, 128):
                        spread[2 * i + p, lane // 128, pl.ds(2 * span[0] + q, size, stride=2), :] = (
                            summed[i * size : (i + 1) * size, lane : lane + 128]
                        )
            for i in range(band):
                for lane in range(0, channels, 128):
                    to = pl.ds(2 * span[0], 2 * size)
                    out[0, 2 * i + p, to, pl.ds(lane, 128)] = (
                        spread[2 * i + p, lane // 128, to].astype(bf16)
                    )

    done = 0
    for c, span in enumerate(spans):
        at = cells(span)

        @pl.when(has_below)
        def _():
            r_copy(c, 0).wait_recv()

        @pl.when(has_above)
        def _():
            r_copy(c, 1).wait_recv()

        acc[pl.ds(band, 2), at] += got[0, :, at].astype(f32)
        acc[pl.ds(0, 2), at] += got[1, :, at].astype(f32)
        for j in range(band + 2):
            place = r * band + j - 1
            mpad[j, pl.ds(PAD + span[0], span[1] - span[0])] = jnp.where(
                (place >= 0) & (place < n_rows * band), acc[j, at], 0.0
            )
        if c == middle - 1 or c == parts - 1:
            end = columns if c == parts - 1 else span[1] - EDGE
            join(mpad, mjoined, (done, end))
            upsample((done, end))
            done = end

    pltpu.make_async_copy(everyone, everyone, stat_send).wait()

    @pl.when(has_next)
    def _():
        for c in range(parts):
            g_copy(2, c).wait_send()

    @pl.when(has_last & has_next)
    def _():
        for c in range(parts):
            x_copy(c).wait_send()
            g_copy(1, c).wait_send()

    @pl.when(has_above)
    def _():
        for c in range(parts):
            r_copy(c, 0).wait_send()

    @pl.when(has_below)
    def _():
        for c in range(parts):
            r_copy(c, 1).wait_send()


def body(
    frames, frame_counts, norm_gain, norm_bias, conv3_weight, conv3_bias, conv2_weight, conv2_bias
):
    n_tm, n_rows = lax.axis_size("tm"), lax.axis_size("rows")
    _, band, columns, channels = frames.shape
    parts = len(cut(columns, 4))
    vmem = pl.BlockSpec(memory_space=pltpu.VMEM)
    hbm = pl.BlockSpec(memory_space=pltpu.HBM)
    dma = pltpu.SemaphoreType.DMA
    return pl.pallas_call(
        functools.partial(kernel, n_tm, n_rows),
        out_shape=pltpu.VMEM((1, 2 * band, 2 * columns, channels), bf16),
        in_specs=[
            hbm
        ] * 8,
        out_specs=vmem,
        scratch_shapes=[
            pltpu.SMEM((n_tm,), jnp.int32),
            pltpu.VMEM(frames.shape, bf16),
            pltpu.VMEM((1, channels), f32),
            pltpu.VMEM((1, channels), f32),
            pltpu.VMEM((1, channels), f32),
            pltpu.VMEM((1, channels), f32),
            pltpu.VMEM((3, 3, 3 * channels, channels), bf16),
            pltpu.VMEM((3, 3, channels, channels), bf16),
            pltpu.VMEM((2, 2, 2, 2 * channels, channels), bf16),
            pltpu.VMEM((band, columns, channels), bf16),
            pltpu.VMEM((band, columns, channels), bf16),
            pltpu.VMEM((3, band, columns, channels), bf16),
            pltpu.VMEM((3, band, columns + 2 * PAD, channels), f32),
            pltpu.VMEM((3, band, columns, 3 * channels), bf16),
            pltpu.VMEM((band + 2, columns, channels), f32),
            pltpu.VMEM((2, 2, columns, channels), bf16),
            pltpu.VMEM((2, 2, columns, channels), bf16),
            pltpu.VMEM((band + 2, columns + 2 * PAD, channels), f32),
            pltpu.VMEM((band + 2, columns, 3 * channels), bf16),
            pltpu.VMEM((2 * band, channels // 128, 2 * columns, 128), f32),
            pltpu.VMEM((n_tm * n_rows, 1, LANES), f32),
            dma((8,)),
            dma((parts,)), dma((parts,)),
            dma((2, parts)), dma((2, parts)),
            dma((parts, 2)), dma((parts, 2)),
            dma, dma,
            pltpu.SemaphoreType.REGULAR((n_tm,)),
        ],
        compiler_params=pltpu.CompilerParams(
            collective_id=0, has_side_effects=True, vmem_limit_bytes=60000000
        ),
        name="decoder_section",
    )(
        frame_counts, frames, norm_gain[None], norm_bias[None],
        conv3_weight.reshape(3, 3, 3 * channels, channels), conv3_bias[None],
        conv2_weight, conv2_bias[None],
    )


def solution(mesh):
    placed = (P("tm", "rows", None, None), P(), P(), P(), P(), P(), P(), P())
    return jax.shard_map(
        body, mesh=mesh, in_specs=placed, out_specs=P("tm", "rows", None, None), check_vma=False
    )
```

```python
import functools

import jax
import jax.numpy as jnp
from jax import lax
from jax.experimental import pallas as pl
from jax.experimental.pallas import tpu as pltpu
from jax.sharding import PartitionSpec as P

GROUPS = 32
norm_eps = 1e-06
EDGE = 16
PAD = 8
LANES = 128
MESH = pl.DeviceIdType.MESH
f32 = jnp.float32
bf16 = jnp.bfloat16


def group_total(value, width):
    channels = value.shape[1]
    lane = lax.broadcasted_iota(jnp.int32, value.shape, 1)
    step = 1
    while step < width:
        up = pltpu.roll(value, step, 1)
        down = pltpu.roll(value, channels - step, 1)
        value = value + jnp.where((lane // step) % 2 == 1, up, down)
        step *= 2
    return value


def cut(columns, parts):
    while parts > 1 and columns % (EDGE * parts) != 0:
        parts -= 1
    step = columns // parts
    return [(i * step, (i + 1) * step) for i in range(parts)]


def pushed(spans, columns):
    ends = [min(b + EDGE, columns) for _, b in spans]
    ends[-1] = columns
    starts = [0] + ends[:-1]
    return list(zip(starts, ends))


def kernel(
    n_tm, n_rows,
    counts_hbm, frames_hbm, gain_hbm, bias_hbm, w3_hbm, b3_hbm, w2_hbm, b2_hbm,
    out,
    counts, frames, gain, bias, b3, b2,
    w3, w2, cw, xsel, xgot, ext, hid, joined, acc, stage, got, mpad, mjoined, spread,
    stats,
    w_sem, sx, rx, sg, rg, sr, rr, stat_send, stat_recv, ready,
):
    slots, band, columns, channels = frames_hbm.shape
    n_all = n_tm * n_rows
    d = lax.axis_index("tm")
    r = lax.axis_index("rows")
    me = d * n_rows + r
    spans = cut(columns, 4)
    arrivals = pushed(spans, columns)
    parts = len(spans)
    middle = (parts + 1) // 2
    runs = [run for run in ((0, middle), (middle, parts)) if run[0] < run[1]]

    load_counts = pltpu.make_async_copy(counts_hbm, counts, w_sem.at[2])
    load_frames = pltpu.make_async_copy(frames_hbm, frames, w_sem.at[3])
    load3 = pltpu.make_async_copy(w3_hbm, w3, w_sem.at[0])
    load2 = pltpu.make_async_copy(w2_hbm, w2, w_sem.at[1])
    small = [
        pltpu.make_async_copy(source, target, w_sem.at[4 + i])
        for i, (source, target) in enumerate(
            ((gain_hbm, gain), (bias_hbm, bias), (b3_hbm, b3), (b2_hbm, b2))
        )
    ]
    barrier = pltpu.get_barrier_semaphore()

    @pl.when(d > 0)
    def _():
        pl.semaphore_signal(barrier, inc=1, device_id=(d - 1, r), device_id_type=MESH)

    load_counts.start()
    load_frames.start()
    load2.start()
    load3.start()
    for load in small:
        load.start()

    has_next, has_last = d < n_tm - 1, d > 0
    has_above, has_below = r > 0, r < n_rows - 1

    def away(rr):
        steps, step = 0, 2
        while step < n_rows:
            steps = steps + (rr // step) % 2
            step *= 2
        return steps

    def rank(dd, rr):
        return (dd + away(rr)) * n_all + dd * n_rows + rr

    my_rank = rank(d, r)

    def each(act):
        def plane(dd, carry):
            for at in range(n_rows):
                act(dd, jnp.int32(at))
            return carry

        lax.fori_loop(0, n_tm, plane, 0)

    def later(dd, rr):
        return rank(dd, rr) > my_rank

    def earlier(dd, rr):
        return rank(dd, rr) < my_rank

    n_later = jnp.int32(0)
    for at_tm in range(n_tm):
        for at_rows in range(n_rows):
            n_later = n_later + later(at_tm, at_rows).astype(jnp.int32)

    def greet(dd, rr):
        @pl.when(later(dd, rr))
        def _():
            pl.semaphore_signal(barrier, inc=1, device_id=(dd, rr), device_id_type=MESH)

    each(greet)
    load_counts.wait()
    load_frames.wait()
    start = jnp.int32(0)
    for i in range(n_tm):
        start = start + jnp.where(i < d, counts[i], 0)
    live = counts[d]
    own_first = start == d

    for row in range(band):
        xsel[row] = jnp.where(own_first, frames[1, row], frames[0, row])

    folds = channels // LANES
    kinds = 2 * folds
    width = channels // GROUPS
    kind_of = lax.broadcasted_iota(jnp.int32, (kinds, LANES), 1) % kinds
    kind_is = kind_of == lax.broadcasted_iota(jnp.int32, (kinds, LANES), 0)
    sums = jnp.zeros((kinds, LANES), f32)
    for slot in range(slots):
        value = frames[slot].astype(f32).reshape(band * columns // 8, 8, channels)
        total = jnp.sum(jnp.sum(value, axis=0), axis=0, keepdims=True)
        square = jnp.sum(jnp.sum(value * value, axis=0), axis=0, keepdims=True)
        parted = [
            value[:, i * LANES : (i + 1) * LANES] for value in (total, square) for i in range(folds)
        ]
        sums = sums + jnp.where(slot < live, jnp.concatenate(parted, axis=0), 0.0)
    sums = jnp.where(kind_is, group_total(sums, width), 0.0)
    stats[me] = jnp.sum(sums, axis=0, keepdims=True)
    pl.semaphore_wait(barrier, n_all - 1 - n_later + has_next.astype(jnp.int32))

    def cells(span):
        return pl.ds(span[0], span[1] - span[0])

    def x_copy(c):
        return pltpu.make_async_remote_copy(
            src_ref=xsel.at[:, cells(arrivals[c])], dst_ref=xgot.at[:, cells(arrivals[c])],
            send_sem=sx.at[c], recv_sem=rx.at[c],
            device_id={"tm": (d + 1) % n_tm}, device_id_type=MESH,
        )

    def g_copy(frame, c):
        return pltpu.make_async_remote_copy(
            src_ref=ext.at[frame, :, cells(arrivals[c])],
            dst_ref=ext.at[frame - 1, :, cells(arrivals[c])],
            send_sem=sg.at[frame - 1, c], recv_sem=rg.at[frame - 1, c],
            device_id={"tm": (d + 1) % n_tm}, device_id_type=MESH,
        )

    def r_copy(c, down):
        return pltpu.make_async_remote_copy(
            src_ref=stage.at[down, :, cells(spans[c])], dst_ref=got.at[down, :, cells(spans[c])],
            send_sem=sr.at[c, down], recv_sem=rr.at[c, down],
            device_id={"rows": (r + (1 if down else n_rows - 1)) % n_rows}, device_id_type=MESH,
        )

    def send_stats(dd, rr):
        pltpu.make_async_remote_copy(
            src_ref=stats.at[me], dst_ref=stats.at[me], send_sem=stat_send, recv_sem=stat_recv,
            device_id=(dd, rr), device_id_type=MESH,
        ).start()

    @pl.when(has_next)
    def _():
        for c in range(parts):
            x_copy(c).start()

    def announce(dd, rr):
        @pl.when(earlier(dd, rr))
        def _():
            pl.semaphore_signal(ready.at[d], inc=1, device_id=(dd, rr), device_id_type=MESH)

    each(announce)

    def stats_down(dd, rr):
        @pl.when(earlier(dd, rr))
        def _():
            send_stats(dd, rr)

    def stats_up(dd):
        ahead = jnp.int32(0)
        for at_rows in range(n_rows):
            ahead = ahead + later(dd, at_rows).astype(jnp.int32)

        @pl.when(ahead > 0)
        def _():
            pl.semaphore_wait(ready.at[dd], ahead)
            for at_rows in range(n_rows):
                @pl.when(later(dd, at_rows))
                def _():
                    send_stats(dd, jnp.int32(at_rows))

    def stats_away(dd, carry):
        @pl.when(dd != d)
        def _():
            stats_up(dd)

        return carry

    each(stats_down)

    load2.wait()
    for phase_row in range(2):
        for tap_row in range(2):
            for phase_col in range(2):
                for tap_col in range(2):
                    rows_of = ((0,), (1, 2)) if phase_row == 0 else ((0, 1), (2,))
                    cols_of = ((0,), (1, 2)) if phase_col == 0 else ((0, 1), (2,))
                    summed = None
                    for a in rows_of[tap_row]:
                        for b in cols_of[tap_col]:
                            part = w2[a, b].astype(f32)
                            summed = part if summed is None else summed + part
                    cw[phase_row, tap_row, phase_col, pl.ds(tap_col * channels, channels), :] = (
                        summed.astype(bf16)
                    )
    load3.wait()

    @pl.when(d < 2)
    def _():
        for k in range(3):
            w3[1, k] = (w3[1, k].astype(f32) + w3[0, k].astype(f32)).astype(bf16)

    for ref in (hid.at[0], hid.at[1], hid.at[2], mpad):
        ref[:, pl.ds(0, PAD)] = jnp.zeros((ref.shape[0], PAD, channels), f32)
        ref[:, pl.ds(PAD + columns, PAD)] = jnp.zeros((ref.shape[0], PAD, channels), f32)

    @pl.when(r == n_rows - 1)
    def _():
        got[0] = jnp.zeros(got.shape[1:], bf16)

    @pl.when(r == 0)
    def _():
        got[1] = jnp.zeros(got.shape[1:], bf16)

    for c in range(parts):
        at = cells(arrivals[c])

        @pl.when(has_last)
        def _():
            x_copy(c).wait_recv()
            ext[2, :, at] = jnp.where(own_first, frames[0, :, at], xgot[:, at])

        @pl.when(d == 0)
        def _():
            ext[2, :, at] = frames[0, :, at]

        if c == 0:
            stats_up(d)
        if c == parts // 4:
            lax.fori_loop(0, n_tm, stats_away, 0)

        @pl.when(d == 0)
        def _():
            x_copy(c).wait_send()

        @pl.when(has_next)
        def _():
            g_copy(2, c).start()

    def pass_on(first, last):
        for c in range(first, last):
            g_copy(2, c).wait_recv()

            @pl.when(has_next)
            def _():
                g_copy(1, c).start()

    @pl.when(has_last)
    def _():
        pass_on(0, parts)

    for load in small:
        load.wait()
    acc[0] = jnp.zeros((columns, channels), f32)
    acc[band + 1] = jnp.zeros((columns, channels), f32)
    acc[pl.ds(1, band)] = ext[2].astype(f32) + b3[...]
    everyone = stats.at[pl.ds(0, n_all - 1)]
    pltpu.make_async_copy(everyone, everyone, stat_recv).wait()
    whole = jnp.where(kind_is, jnp.sum(stats[...], axis=0), 0.0)
    whole = group_total(whole, width) / float(n_all * band * columns * width * (width // kinds))
    mean, mean_square = (
        jnp.concatenate([whole[i + k : i + k + 1] for i in range(folds)], axis=1) for k in (0, folds)
    )
    inverse = lax.rsqrt(mean_square - mean * mean + norm_eps)
    scale = inverse * gain[...]
    shift = bias[...] - mean * inverse * gain[...]

    def hide(frame, span):
        value = ext[jnp.maximum(frame, 2 - d), :, cells(span)].astype(f32) * scale + shift
        value = 0.5 * value * (1.0 + jnp.tanh(0.5 * value))
        hid[frame, :, pl.ds(PAD + span[0], span[1] - span[0])] = value

    def join(source, target, span):
        for i in range(3):
            target[:, cells(span), pl.ds(i * channels, channels)] = (
                source[:, pl.ds(PAD + span[0] + i - 1, span[1] - span[0])].astype(bf16)
            )

    def taps(frame, held, span):
        size = span[1] - span[0]
        value = joined[held, :, cells(span), :].reshape(band * size, 3 * channels)
        for k in range(3):
            acc[pl.ds(2 - k, band), cells(span)] += jnp.dot(
                value, w3[frame, k], preferred_element_type=f32
            ).reshape(band, size, channels)

    def send_edges(first, last):
        at = cells((spans[first][0], spans[last - 1][1]))
        stage[0, :, at] = acc[pl.ds(0, 2), at].astype(bf16)
        stage[1, :, at] = acc[pl.ds(band, 2), at].astype(bf16)

        @pl.when(has_above)
        def _():
            for c in range(first, last):
                r_copy(c, 0).start()

        @pl.when(has_below)
        def _():
            for c in range(first, last):
                r_copy(c, 1).start()

    every = (0, columns)
    hide(2, every)
    join(hid.at[2], joined.at[2], every)
    taps(2, 2, every)

    def covered(spans, run):
        return spans[run[0]][0], spans[run[1] - 1][1]

    @pl.when(d < 2)
    def _():
        for run in runs:
            hide(1, covered(arrivals, run))
            join(hid.at[1], joined.at[1], covered(spans, run))
            taps(1, 1, covered(spans, run))
            send_edges(*run)

    @pl.when(d >= 2)
    def _():
        hide(1, every)
        join(hid.at[1], joined.at[1], every)
        taps(1, 1, every)
        for run in runs:
            for c in range(*run):
                g_copy(1, c).wait_recv()
            hide(0, covered(arrivals, run))
            join(hid.at[0], joined.at[0], covered(spans, run))
            taps(0, 0, covered(spans, run))
            send_edges(*run)

    def upsample(span):
        size = span[1] - span[0]
        for p in range(2):
            for q in range(2):
                summed = b2[...]
                for t in range(2):
                    value = mjoined[pl.ds(p + t, band), cells(span), pl.ds(q * channels, 2 * channels)]
                    summed = summed + jnp.dot(
                        value.reshape(band * size, 2 * channels), cw[p, t, q],
                        preferred_element_type=f32,
                    )
                for i in range(band):
                    for lane in range(0, channels, 128):
                        spread[2 * i + p, lane // 128, pl.ds(2 * span[0] + q, size, stride=2), :] = (
                            summed[i * size : (i + 1) * size, lane : lane + 128]
                        )
            for i in range(band):
                for lane in range(0, channels, 128):
                    to = pl.ds(2 * span[0], 2 * size)
                    out[0, 2 * i + p, to, pl.ds(lane, 128)] = (
                        spread[2 * i + p, lane // 128, to].astype(bf16)
                    )

    done = 0
    for c, span in enumerate(spans):
        at = cells(span)

        @pl.when(has_below)
        def _():
            r_copy(c, 0).wait_recv()

        @pl.when(has_above)
        def _():
            r_copy(c, 1).wait_recv()

        acc[pl.ds(band, 2), at] += got[0, :, at].astype(f32)
        acc[pl.ds(0, 2), at] += got[1, :, at].astype(f32)
        for j in range(band + 2):
            place = r * band + j - 1
            mpad[j, pl.ds(PAD + span[0], span[1] - span[0])] = jnp.where(
                (place >= 0) & (place < n_rows * band), acc[j, at], 0.0
            )
        if c == middle - 1 or c == parts - 1:
            end = columns if c == parts - 1 else span[1] - EDGE
            join(mpad, mjoined, (done, end))
            upsample((done, end))
            done = end

    pltpu.make_async_copy(everyone, everyone, stat_send).wait()

    @pl.when(has_next)
    def _():
        for c in range(parts):
            g_copy(2, c).wait_send()

    @pl.when(has_last & has_next)
    def _():
        for c in range(parts):
            x_copy(c).wait_send()
            g_copy(1, c).wait_send()

    @pl.when(has_above)
    def _():
        for c in range(parts):
            r_copy(c, 0).wait_send()

    @pl.when(has_below)
    def _():
        for c in range(parts):
            r_copy(c, 1).wait_send()


def body(
    frames, frame_counts, norm_gain, norm_bias, conv3_weight, conv3_bias, conv2_weight, conv2_bias
):
    n_tm, n_rows = lax.axis_size("tm"), lax.axis_size("rows")
    _, band, columns, channels = frames.shape
    parts = len(cut(columns, 4))
    vmem = pl.BlockSpec(memory_space=pltpu.VMEM)
    hbm = pl.BlockSpec(memory_space=pltpu.HBM)
    dma = pltpu.SemaphoreType.DMA
    return pl.pallas_call(
        functools.partial(kernel, n_tm, n_rows),
        out_shape=pltpu.VMEM((1, 2 * band, 2 * columns, channels), bf16),
        in_specs=[
            hbm
        ] * 8,
        out_specs=vmem,
        scratch_shapes=[
            pltpu.SMEM((n_tm,), jnp.int32),
            pltpu.VMEM(frames.shape, bf16),
            pltpu.VMEM((1, channels), f32),
            pltpu.VMEM((1, channels), f32),
            pltpu.VMEM((1, channels), f32),
            pltpu.VMEM((1, channels), f32),
            pltpu.VMEM((3, 3, 3 * channels, channels), bf16),
            pltpu.VMEM((3, 3, channels, channels), bf16),
            pltpu.VMEM((2, 2, 2, 2 * channels, channels), bf16),
            pltpu.VMEM((band, columns, channels), bf16),
            pltpu.VMEM((band, columns, channels), bf16),
            pltpu.VMEM((3, band, columns, channels), bf16),
            pltpu.VMEM((3, band, columns + 2 * PAD, channels), f32),
            pltpu.VMEM((3, band, columns, 3 * channels), bf16),
            pltpu.VMEM((band + 2, columns, channels), f32),
            pltpu.VMEM((2, 2, columns, channels), bf16),
            pltpu.VMEM((2, 2, columns, channels), bf16),
            pltpu.VMEM((band + 2, columns + 2 * PAD, channels), f32),
            pltpu.VMEM((band + 2, columns, 3 * channels), bf16),
            pltpu.VMEM((2 * band, channels // 128, 2 * columns, 128), f32),
            pltpu.VMEM((n_tm * n_rows, 1, LANES), f32),
            dma((8,)),
            dma((parts,)), dma((parts,)),
            dma((2, parts)), dma((2, parts)),
            dma((parts, 2)), dma((parts, 2)),
            dma, dma,
            pltpu.SemaphoreType.REGULAR((n_tm,)),
        ],
        compiler_params=pltpu.CompilerParams(
            collective_id=0, has_side_effects=True, vmem_limit_bytes=60000000
        ),
        name="decoder_section",
    )(
        frame_counts, frames, norm_gain[None], norm_bias[None],
        conv3_weight.reshape(3, 3, 3 * channels, channels), conv3_bias[None],
        conv2_weight, conv2_bias[None],
    )


def solution(mesh):
    placed = (P("tm", "rows", None, None), P(), P(), P(), P(), P(), P(), P())
    return jax.shard_map(
        body, mesh=mesh, in_specs=placed, out_specs=P("tm", "rows", None, None), check_vma=False
    )
```

```python
import functools

import jax
import jax.numpy as jnp
from jax import lax
from jax.experimental import pallas as pl
from jax.experimental.pallas import tpu as pltpu
from jax.sharding import PartitionSpec as P

GROUPS = 32
norm_eps = 1e-06
EDGE = 16
PAD = 8
LANES = 128
MESH = pl.DeviceIdType.MESH
f32 = jnp.float32
bf16 = jnp.bfloat16


def group_total(value, width):
    channels = value.shape[1]
    lane = lax.broadcasted_iota(jnp.int32, value.shape, 1)
    step = 1
    while step < width:
        up = pltpu.roll(value, step, 1)
        down = pltpu.roll(value, channels - step, 1)
        value = value + jnp.where((lane // step) % 2 == 1, up, down)
        step *= 2
    return value


def cut(columns, parts):
    while parts > 1 and columns % (EDGE * parts) != 0:
        parts -= 1
    step = columns // parts
    return [(i * step, (i + 1) * step) for i in range(parts)]


def pushed(spans, columns):
    ends = [min(b + EDGE, columns) for _, b in spans]
    ends[-1] = columns
    starts = [0] + ends[:-1]
    return list(zip(starts, ends))


def kernel(
    n_tm, n_rows,
    counts_hbm, frames_hbm, gain_hbm, bias_hbm, w3_hbm, b3_hbm, w2_hbm, b2_hbm,
    out,
    counts, frames, gain, bias, b3, b2,
    w3, w2, cw, xsel, xgot, ext, hid, joined, acc, stage, got, mpad, mjoined, spread,
    stats,
    w_sem, sx, rx, sg, rg, sr, rr, stat_send, stat_recv, ready, turn,
):
    slots, band, columns, channels = frames_hbm.shape
    n_all = n_tm * n_rows
    d = lax.axis_index("tm")
    r = lax.axis_index("rows")
    me = d * n_rows + r
    spans = cut(columns, 4)
    arrivals = pushed(spans, columns)
    parts = len(spans)
    middle = (parts + 1) // 2
    runs = [run for run in ((0, middle), (middle, parts)) if run[0] < run[1]]

    load_counts = pltpu.make_async_copy(counts_hbm, counts, w_sem.at[2])
    load_frames = pltpu.make_async_copy(frames_hbm, frames, w_sem.at[3])
    load3 = pltpu.make_async_copy(w3_hbm, w3, w_sem.at[0])
    load2 = pltpu.make_async_copy(w2_hbm, w2, w_sem.at[1])
    small = [
        pltpu.make_async_copy(source, target, w_sem.at[4 + i])
        for i, (source, target) in enumerate(
            ((gain_hbm, gain), (bias_hbm, bias), (b3_hbm, b3), (b2_hbm, b2))
        )
    ]
    barrier = pltpu.get_barrier_semaphore()

    @pl.when(d > 0)
    def _():
        pl.semaphore_signal(barrier, inc=1, device_id=(d - 1, r), device_id_type=MESH)

    load_counts.start()
    load_frames.start()
    load2.start()
    load3.start()
    for load in small:
        load.start()

    has_next, has_last = d < n_tm - 1, d > 0
    has_above, has_below = r > 0, r < n_rows - 1

    def away(rr):
        steps, step = 0, 2
        while step < n_rows:
            steps = steps + (rr // step) % 2
            step *= 2
        return steps

    def rank(dd, rr):
        return (dd + away(rr)) * n_all + dd * n_rows + rr + 1 - 2 * (rr % 2)

    my_rank = rank(d, r)

    def each(act):
        def plane(dd, carry):
            for at in range(n_rows):
                act(dd, jnp.int32(at))
            return carry

        lax.fori_loop(0, n_tm, plane, 0)

    def later(dd, rr):
        return rank(dd, rr) > my_rank

    def earlier(dd, rr):
        return rank(dd, rr) < my_rank

    n_later = jnp.int32(0)
    for at_tm in range(n_tm):
        for at_rows in range(n_rows):
            n_later = n_later + later(at_tm, at_rows).astype(jnp.int32)

    def greet(dd, rr):
        @pl.when(later(dd, rr))
        def _():
            pl.semaphore_signal(barrier, inc=1, device_id=(dd, rr), device_id_type=MESH)

    each(greet)
    load_counts.wait()
    load_frames.wait()
    start = jnp.int32(0)
    for i in range(n_tm):
        start = start + jnp.where(i < d, counts[i], 0)
    live = counts[d]
    own_first = start == d

    for row in range(band):
        xsel[row] = jnp.where(own_first, frames[1, row], frames[0, row])

    folds = channels // LANES
    kinds = 2 * folds
    width = channels // GROUPS
    kind_of = lax.broadcasted_iota(jnp.int32, (kinds, LANES), 1) % kinds
    kind_is = kind_of == lax.broadcasted_iota(jnp.int32, (kinds, LANES), 0)
    sums = jnp.zeros((kinds, LANES), f32)
    for slot in range(slots):
        value = frames[slot].astype(f32).reshape(band * columns // 8, 8, channels)
        total = jnp.sum(jnp.sum(value, axis=0), axis=0, keepdims=True)
        square = jnp.sum(jnp.sum(value * value, axis=0), axis=0, keepdims=True)
        parted = [
            value[:, i * LANES : (i + 1) * LANES] for value in (total, square) for i in range(folds)
        ]
        sums = sums + jnp.where(slot < live, jnp.concatenate(parted, axis=0), 0.0)
    sums = jnp.where(kind_is, group_total(sums, width), 0.0)
    stats[me] = jnp.sum(sums, axis=0, keepdims=True)
    pl.semaphore_wait(barrier, n_all - 1 - n_later + has_next.astype(jnp.int32))

    def cells(span):
        return pl.ds(span[0], span[1] - span[0])

    def x_copy(c):
        return pltpu.make_async_remote_copy(
            src_ref=xsel.at[:, cells(arrivals[c])], dst_ref=xgot.at[:, cells(arrivals[c])],
            send_sem=sx.at[c], recv_sem=rx.at[c],
            device_id={"tm": (d + 1) % n_tm}, device_id_type=MESH,
        )

    def g_copy(frame, c):
        return pltpu.make_async_remote_copy(
            src_ref=ext.at[frame, :, cells(arrivals[c])],
            dst_ref=ext.at[frame - 1, :, cells(arrivals[c])],
            send_sem=sg.at[frame - 1, c], recv_sem=rg.at[frame - 1, c],
            device_id={"tm": (d + 1) % n_tm}, device_id_type=MESH,
        )

    def r_copy(c, down):
        return pltpu.make_async_remote_copy(
            src_ref=stage.at[down, :, cells(spans[c])], dst_ref=got.at[down, :, cells(spans[c])],
            send_sem=sr.at[c, down], recv_sem=rr.at[c, down],
            device_id={"rows": (r + (1 if down else n_rows - 1)) % n_rows}, device_id_type=MESH,
        )

    def send_stats(dd, rr):
        pltpu.make_async_remote_copy(
            src_ref=stats.at[me], dst_ref=stats.at[me], send_sem=stat_send, recv_sem=stat_recv,
            device_id=(dd, rr), device_id_type=MESH,
        ).start()

    gives = has_next & (r % 2 == 0)
    takes = has_next & (r % 2 == 1)

    @pl.when(takes)
    def _():
        x_copy(0).start()
        pl.semaphore_wait(turn, 1)
        for c in range(1, parts):
            x_copy(c).start()

    @pl.when(gives)
    def _():
        for c in range(parts):
            x_copy(c).start()
        pl.semaphore_signal(turn, inc=1, device_id=(d, r + 1), device_id_type=MESH)

    def announce(dd, rr):
        @pl.when(earlier(dd, rr))
        def _():
            pl.semaphore_signal(ready.at[d], inc=1, device_id=(dd, rr), device_id_type=MESH)

    each(announce)

    def stats_down(dd, rr):
        @pl.when(earlier(dd, rr))
        def _():
            send_stats(dd, rr)

    def stats_up(dd):
        ahead = jnp.int32(0)
        for at_rows in range(n_rows):
            ahead = ahead + later(dd, at_rows).astype(jnp.int32)

        @pl.when(ahead > 0)
        def _():
            pl.semaphore_wait(ready.at[dd], ahead)
            for at_rows in range(n_rows):
                @pl.when(later(dd, at_rows))
                def _():
                    send_stats(dd, jnp.int32(at_rows))

    def stats_away(dd, carry):
        @pl.when(dd != d)
        def _():
            stats_up(dd)

        return carry

    each(stats_down)

    load2.wait()
    for phase_row in range(2):
        for tap_row in range(2):
            for phase_col in range(2):
                for tap_col in range(2):
                    rows_of = ((0,), (1, 2)) if phase_row == 0 else ((0, 1), (2,))
                    cols_of = ((0,), (1, 2)) if phase_col == 0 else ((0, 1), (2,))
                    summed = None
                    for a in rows_of[tap_row]:
                        for b in cols_of[tap_col]:
                            part = w2[a, b].astype(f32)
                            summed = part if summed is None else summed + part
                    cw[phase_row, tap_row, phase_col, pl.ds(tap_col * channels, channels), :] = (
                        summed.astype(bf16)
                    )
    load3.wait()

    @pl.when(d < 2)
    def _():
        for k in range(3):
            w3[1, k] = (w3[1, k].astype(f32) + w3[0, k].astype(f32)).astype(bf16)

    for ref in (hid.at[0], hid.at[1], hid.at[2], mpad):
        ref[:, pl.ds(0, PAD)] = jnp.zeros((ref.shape[0], PAD, channels), f32)
        ref[:, pl.ds(PAD + columns, PAD)] = jnp.zeros((ref.shape[0], PAD, channels), f32)

    @pl.when(r == n_rows - 1)
    def _():
        got[0] = jnp.zeros(got.shape[1:], bf16)

    @pl.when(r == 0)
    def _():
        got[1] = jnp.zeros(got.shape[1:], bf16)

    for c in range(parts):
        at = cells(arrivals[c])

        @pl.when(has_last)
        def _():
            x_copy(c).wait_recv()
            ext[2, :, at] = jnp.where(own_first, frames[0, :, at], xgot[:, at])

        @pl.when(d == 0)
        def _():
            ext[2, :, at] = frames[0, :, at]

        if c == 0:
            stats_up(d)
        if c == parts // 4:
            lax.fori_loop(0, n_tm, stats_away, 0)

        @pl.when(d == 0)
        def _():
            x_copy(c).wait_send()

        @pl.when(has_next)
        def _():
            g_copy(2, c).start()

    def pass_on(first, last):
        for c in range(first, last):
            g_copy(2, c).wait_recv()

            @pl.when(has_next)
            def _():
                g_copy(1, c).start()

    @pl.when(has_last)
    def _():
        pass_on(0, parts)

    for load in small:
        load.wait()
    acc[0] = jnp.zeros((columns, channels), f32)
    acc[band + 1] = jnp.zeros((columns, channels), f32)
    acc[pl.ds(1, band)] = ext[2].astype(f32) + b3[...]
    everyone = stats.at[pl.ds(0, n_all - 1)]
    pltpu.make_async_copy(everyone, everyone, stat_recv).wait()
    whole = jnp.where(kind_is, jnp.sum(stats[...], axis=0), 0.0)
    whole = group_total(whole, width) / float(n_all * band * columns * width * (width // kinds))
    mean, mean_square = (
        jnp.concatenate([whole[i + k : i + k + 1] for i in range(folds)], axis=1) for k in (0, folds)
    )
    inverse = lax.rsqrt(mean_square - mean * mean + norm_eps)
    scale = inverse * gain[...]
    shift = bias[...] - mean * inverse * gain[...]

    def hide(frame, span):
        value = ext[jnp.maximum(frame, 2 - d), :, cells(span)].astype(f32) * scale + shift
        value = 0.5 * value * (1.0 + jnp.tanh(0.5 * value))
        hid[frame, :, pl.ds(PAD + span[0], span[1] - span[0])] = value

    def join(source, target, span):
        for i in range(3):
            target[:, cells(span), pl.ds(i * channels, channels)] = (
                source[:, pl.ds(PAD + span[0] + i - 1, span[1] - span[0])].astype(bf16)
            )

    def taps(frame, held, span):
        size = span[1] - span[0]
        value = joined[held, :, cells(span), :].reshape(band * size, 3 * channels)
        for k in range(3):
            acc[pl.ds(2 - k, band), cells(span)] += jnp.dot(
                value, w3[frame, k], preferred_element_type=f32
            ).reshape(band, size, channels)

    def send_edges(first, last):
        at = cells((spans[first][0], spans[last - 1][1]))
        stage[0, :, at] = acc[pl.ds(0, 2), at].astype(bf16)
        stage[1, :, at] = acc[pl.ds(band, 2), at].astype(bf16)

        @pl.when(has_above)
        def _():
            for c in range(first, last):
                r_copy(c, 0).start()

        @pl.when(has_below)
        def _():
            for c in range(first, last):
                r_copy(c, 1).start()

    every = (0, columns)
    hide(2, every)
    join(hid.at[2], joined.at[2], every)
    taps(2, 2, every)

    def covered(spans, run):
        return spans[run[0]][0], spans[run[1] - 1][1]

    @pl.when(d < 2)
    def _():
        for run in runs:
            hide(1, covered(arrivals, run))
            join(hid.at[1], joined.at[1], covered(spans, run))
            taps(1, 1, covered(spans, run))
            send_edges(*run)

    @pl.when(d >= 2)
    def _():
        hide(1, every)
        join(hid.at[1], joined.at[1], every)
        taps(1, 1, every)
        for run in runs:
            for c in range(*run):
                g_copy(1, c).wait_recv()
            hide(0, covered(arrivals, run))
            join(hid.at[0], joined.at[0], covered(spans, run))
            taps(0, 0, covered(spans, run))
            send_edges(*run)

    def upsample(span):
        size = span[1] - span[0]
        for p in range(2):
            for q in range(2):
                summed = b2[...]
                for t in range(2):
                    value = mjoined[pl.ds(p + t, band), cells(span), pl.ds(q * channels, 2 * channels)]
                    summed = summed + jnp.dot(
                        value.reshape(band * size, 2 * channels), cw[p, t, q],
                        preferred_element_type=f32,
                    )
                for i in range(band):
                    for lane in range(0, channels, 128):
                        spread[2 * i + p, lane // 128, pl.ds(2 * span[0] + q, size, stride=2), :] = (
                            summed[i * size : (i + 1) * size, lane : lane + 128]
                        )
            for i in range(band):
                for lane in range(0, channels, 128):
                    to = pl.ds(2 * span[0], 2 * size)
                    out[0, 2 * i + p, to, pl.ds(lane, 128)] = (
                        spread[2 * i + p, lane // 128, to].astype(bf16)
                    )

    done = 0
    for c, span in enumerate(spans):
        at = cells(span)

        @pl.when(has_below)
        def _():
            r_copy(c, 0).wait_recv()

        @pl.when(has_above)
        def _():
            r_copy(c, 1).wait_recv()

        acc[pl.ds(band, 2), at] += got[0, :, at].astype(f32)
        acc[pl.ds(0, 2), at] += got[1, :, at].astype(f32)
        for j in range(band + 2):
            place = r * band + j - 1
            mpad[j, pl.ds(PAD + span[0], span[1] - span[0])] = jnp.where(
                (place >= 0) & (place < n_rows * band), acc[j, at], 0.0
            )
        if c == middle - 1 or c == parts - 1:
            end = columns if c == parts - 1 else span[1] - EDGE
            join(mpad, mjoined, (done, end))
            upsample((done, end))
            done = end

    pltpu.make_async_copy(everyone, everyone, stat_send).wait()

    @pl.when(has_next)
    def _():
        for c in range(parts):
            g_copy(2, c).wait_send()

    @pl.when(has_last & has_next)
    def _():
        for c in range(parts):
            x_copy(c).wait_send()
            g_copy(1, c).wait_send()

    @pl.when(has_above)
    def _():
        for c in range(parts):
            r_copy(c, 0).wait_send()

    @pl.when(has_below)
    def _():
        for c in range(parts):
            r_copy(c, 1).wait_send()


def body(
    frames, frame_counts, norm_gain, norm_bias, conv3_weight, conv3_bias, conv2_weight, conv2_bias
):
    n_tm, n_rows = lax.axis_size("tm"), lax.axis_size("rows")
    _, band, columns, channels = frames.shape
    parts = len(cut(columns, 4))
    vmem = pl.BlockSpec(memory_space=pltpu.VMEM)
    hbm = pl.BlockSpec(memory_space=pltpu.HBM)
    dma = pltpu.SemaphoreType.DMA
    return pl.pallas_call(
        functools.partial(kernel, n_tm, n_rows),
        out_shape=pltpu.VMEM((1, 2 * band, 2 * columns, channels), bf16),
        in_specs=[
            hbm
        ] * 8,
        out_specs=vmem,
        scratch_shapes=[
            pltpu.SMEM((n_tm,), jnp.int32),
            pltpu.VMEM(frames.shape, bf16),
            pltpu.VMEM((1, channels), f32),
            pltpu.VMEM((1, channels), f32),
            pltpu.VMEM((1, channels), f32),
            pltpu.VMEM((1, channels), f32),
            pltpu.VMEM((3, 3, 3 * channels, channels), bf16),
            pltpu.VMEM((3, 3, channels, channels), bf16),
            pltpu.VMEM((2, 2, 2, 2 * channels, channels), bf16),
            pltpu.VMEM((band, columns, channels), bf16),
            pltpu.VMEM((band, columns, channels), bf16),
            pltpu.VMEM((3, band, columns, channels), bf16),
            pltpu.VMEM((3, band, columns + 2 * PAD, channels), f32),
            pltpu.VMEM((3, band, columns, 3 * channels), bf16),
            pltpu.VMEM((band + 2, columns, channels), f32),
            pltpu.VMEM((2, 2, columns, channels), bf16),
            pltpu.VMEM((2, 2, columns, channels), bf16),
            pltpu.VMEM((band + 2, columns + 2 * PAD, channels), f32),
            pltpu.VMEM((band + 2, columns, 3 * channels), bf16),
            pltpu.VMEM((2 * band, channels // 128, 2 * columns, 128), f32),
            pltpu.VMEM((n_tm * n_rows, 1, LANES), f32),
            dma((8,)),
            dma((parts,)), dma((parts,)),
            dma((2, parts)), dma((2, parts)),
            dma((parts, 2)), dma((parts, 2)),
            dma, dma,
            pltpu.SemaphoreType.REGULAR((n_tm,)), pltpu.SemaphoreType.REGULAR,
        ],
        compiler_params=pltpu.CompilerParams(
            collective_id=0, has_side_effects=True, vmem_limit_bytes=60000000
        ),
        name="decoder_section",
    )(
        frame_counts, frames, norm_gain[None], norm_bias[None],
        conv3_weight.reshape(3, 3, 3 * channels, channels), conv3_bias[None],
        conv2_weight, conv2_bias[None],
    )


def solution(mesh):
    placed = (P("tm", "rows", None, None), P(), P(), P(), P(), P(), P(), P())
    return jax.shard_map(
        body, mesh=mesh, in_specs=placed, out_specs=P("tm", "rows", None, None), check_vma=False
    )
```
